256 devices in a mesh: gx: 4 (over y), gy: 8 (over x, core), gz: 8 (over z).
Axes of the slice: x: 4, y: 4, z: 8, core: 2. Of those that a mesh axis runs over, the one named last changes fastest.
Arguments:
- gradient: float32 [4, 8, 8, 16, 512], P('gx', 'gy', 'gz'), may hold values from -60 to 60
- local_schur: bfloat16 [4, 8, 8, 2048, 2048], P('gx', 'gy', 'gz'), may hold values from -1 to 4
- inverse_rows: bfloat16 [4, 8, 8, 512, 2048], P('gx', 'gy', 'gz'), may hold values from -0.1 to 0.6
- face_maps: int32 [4, 8, 8, 6, 256], P('gx', 'gy', 'gz'), may hold values from 0 to 511, as said below
Outputs:
- adjoint: float32 [4, 8, 8, 16, 512], P('gx', 'gy', 'gz')
- residual_ratio: float32 [16], replicated
The draws below stay inside these ranges and needn't reach their ends.
Inputs may be any that keep to these rules, and one draw needn't show every extreme that they name: `face_maps`: for each subdomain and face, 256 distinct owned rows of the neighbour across that face.
All inputs are finite; a program needn't handle non-finite values.
Results may differ from the reference program's by a relative error of at most 0.0038.
Values may be sent and summed in bfloat16 or wider, within the bound.
No kernel may reach another device: no remote copies, remote signals or barrier semaphores. Data moves between devices by JAX's collectives and lax.ppermute only.
A program may use at most 64 MiB of HBM per device.

```python
import math
import jax
import jax.numpy as jnp
from jax import lax

M = 2048
OWN = 512
RHS = 16
ITERS = 3
FACE = 256
SX = 4
SY = 8
SZ = 8


def device_ramp(highest):
    devices_n = SX * SY * SZ
    flat_ids = jnp.arange(devices_n, dtype=jnp.float32).reshape(SX, SY, SZ, 1, 1)
    return 1.0 + (highest - 1.0) * flat_ids / max(devices_n - 1, 1)


def draw_gradient(key, part):
    subkeys = jax.random.split(jax.random.fold_in(key, 11), 3)
    shape = (SX, SY, SZ, RHS, OWN)
    row_scale = jnp.exp(jax.random.uniform(subkeys[1], (SX, SY, SZ, 1, OWN), jnp.float32, math.log(0.3), math.log(3.0)))
    rhs_scale = jnp.exp(jax.random.uniform(subkeys[2], (1, 1, 1, RHS, 1), jnp.float32, math.log(0.5), math.log(1.5)))
    base_vals = jnp.clip(jax.random.normal(subkeys[0], shape, jnp.float32), -4.0, 4.0)
    ramp_vals = device_ramp(3.0)
    return base_vals * row_scale * rhs_scale * ramp_vals


def draw_local_schur(key, part):
    subkeys = jax.random.split(jax.random.fold_in(key, 23), 2)
    shape = (SX, SY, SZ, M, M)
    sigma = 0.6 / math.sqrt(M)
    noise = jnp.clip(jax.random.normal(subkeys[0], shape, jnp.float32), -4.0, 4.0) * sigma
    diagonal = jax.random.uniform(subkeys[1], (SX, SY, SZ, 1, M), jnp.float32, 1.0, 3.0)
    identity = (jnp.arange(M)[:, None] == jnp.arange(M)[None, :]).astype(jnp.float32)
    return (noise + diagonal * identity).astype(jnp.bfloat16)


def draw_inverse_rows(key, part):
    subkeys = jax.random.split(jax.random.fold_in(key, 37), 2)
    shape = (SX, SY, SZ, OWN, M)
    sigma = 0.1 / math.sqrt(M)
    noise = jnp.clip(jax.random.normal(subkeys[0], shape, jnp.float32), -4.0, 4.0) * sigma
    diagonal = jnp.exp(jax.random.uniform(subkeys[1], (SX, SY, SZ, OWN, 1), jnp.float32, math.log(0.1), math.log(0.5)))
    identity = (jnp.arange(OWN)[:, None] == jnp.arange(M)[None, :]).astype(jnp.float32)
    return (noise + diagonal * identity).astype(jnp.bfloat16)


def draw_face_maps(key, part):
    scores = jax.random.randint(jax.random.fold_in(key, 53), (SX, SY, SZ, 6, OWN), 0, 1 << 20, jnp.int32)
    scores = scores * OWN + jnp.arange(OWN, dtype=jnp.int32)
    return jnp.argsort(scores, axis=-1)[..., :FACE].astype(jnp.int32)


def setup_inputs(seed: int = 0) -> dict:
    streams_of = jax.random.split(jax.random.key(seed), 5)
    gradient = draw_gradient(jax.random.fold_in(streams_of[4], 71), 0)
    local_schur = draw_local_schur(jax.random.fold_in(streams_of[4], 71), 0)
    inverse_rows = draw_inverse_rows(jax.random.fold_in(streams_of[4], 71), 0)
    face_maps = draw_face_maps(jax.random.fold_in(streams_of[4], 71), 0)
    return {"gradient": gradient, "local_schur": local_schur, "inverse_rows": inverse_rows, "face_maps": face_maps}


EPSILON = 1e-06

def across(values, facing):
    dimension = facing // 2
    widths = [(0, 0)] * values.ndim
    extent = values.shape[dimension]
    if facing % 2 == 0:
        widths[dimension] = (1, 0)
        return lax.slice_in_dim(jnp.pad(values, widths), 0, extent, axis=dimension)
    widths[dimension] = (0, 1)
    return lax.slice_in_dim(jnp.pad(values, widths), 1, extent + 1, axis=dimension)

def flatten_grid(values):
    return values.reshape((-1,) + values.shape[3:])

def take_rows(face_block, row_ids):
    return jnp.take(face_block, row_ids, axis=1)

def add_rows(face_block, row_ids, addition):
    return face_block.at[:, row_ids].add(addition)

def multiply_pair(operands):
    return jnp.dot(operands[0], operands[1], preferred_element_type=jnp.float32)

def assemble(products, face_maps):
    owned = products.shape[-1] - 6 * FACE
    result = flatten_grid(products[..., :owned])
    for facing in range(6):
        offset = owned + (facing ^ 1) * FACE
        face_block = across(products[..., offset:offset + FACE], facing)
        row_ids = across(face_maps[..., facing ^ 1, :], facing)
        result = jax.vmap(add_rows)(result, flatten_grid(row_ids), flatten_grid(face_block))
    return result.reshape(products.shape[:-1] + (owned,))

def operator(values, face_maps, local_schur):
    rounded = values.astype(jnp.bfloat16)
    ghosts = [jax.vmap(take_rows)(flatten_grid(across(rounded, facing)), flatten_grid(face_maps[..., facing, :])) for facing in range(6)]
    intersected = jnp.concatenate([flatten_grid(rounded)] + ghosts, axis=2)
    products = lax.map(multiply_pair, (intersected, flatten_grid(local_schur)))
    return assemble(products.reshape(values.shape[:3] + products.shape[1:]), face_maps)

def precondition(values, face_maps, inverse_rows):
    rounded = flatten_grid(values.astype(jnp.bfloat16))
    products = lax.map(multiply_pair, (rounded, flatten_grid(inverse_rows)))
    return assemble(products.reshape(values.shape[:3] + products.shape[1:]), face_maps)

def inner_sum(left_side, right_side):
    return lax.optimization_barrier(jnp.sum(left_side * right_side, axis=(0, 1, 2, 4)))

def rotate_solve(columns, beta_norm):
    num_cols = len(columns)
    rhs_vec = [beta_norm] + [jnp.zeros_like(beta_norm) for unused in range(num_cols)]
    cosines = []
    sines = []
    triangle = []
    for section in range(num_cols):
        column = [columns[section][row_at] for row_at in range(section + 2)]
        for earlier in range(section):
            rotated_a = cosines[earlier] * column[earlier] + sines[earlier] * column[earlier + 1]
            rotated_b = -sines[earlier] * column[earlier] + cosines[earlier] * column[earlier + 1]
            column[earlier] = rotated_a
            column[earlier + 1] = rotated_b
        radius = jnp.sqrt(column[section] * column[section] + column[section + 1] * column[section + 1])
        cosine = column[section] / radius
        sine_val = column[section + 1] / radius
        column[section] = radius
        cosines.append(cosine)
        sines.append(sine_val)
        rhs_vec[section + 1] = -sine_val * rhs_vec[section]
        rhs_vec[section] = cosine * rhs_vec[section]
        triangle.append(column[:section + 1])
    coeffs = [None] * num_cols
    for section in reversed(range(num_cols)):
        running = rhs_vec[section]
        for onward in range(section + 1, num_cols):
            running = running - triangle[onward][section] * coeffs[onward]
        coeffs[section] = running / triangle[section][section]
    return (coeffs, jnp.abs(rhs_vec[num_cols]))

def reference(gradient, local_schur, inverse_rows, face_maps):
    beta_norm = jnp.sqrt(inner_sum(gradient, gradient) + EPSILON)
    krylov = [gradient / beta_norm[:, None]]
    directions = []
    columns = []
    for section in range(ITERS):
        prepared = precondition(krylov[section], face_maps, inverse_rows)
        directions.append(prepared)
        applied = operator(prepared, face_maps, local_schur)
        coeffs = [inner_sum(vector, applied) for vector in krylov]
        residue = applied
        for position in range(section + 1):
            residue = residue - coeffs[position][:, None] * krylov[position]
        height = jnp.sqrt(inner_sum(residue, residue) + EPSILON)
        columns.append(coeffs + [height])
        if section + 1 < ITERS:
            krylov.append(residue / height[:, None])
    weights, remainder = rotate_solve(columns, beta_norm)
    adjoint = weights[0][:, None] * directions[0]
    for position in range(1, ITERS):
        adjoint = adjoint + weights[position][:, None] * directions[position]
    return (adjoint, remainder / beta_norm)
```

```python
import functools

import jax
import jax.numpy as jnp
from jax import lax
from jax.experimental import pallas as pl
from jax.experimental.pallas import tpu as pltpu
from jax.sharding import PartitionSpec as P

ITERS = 3
EPSILON = 1e-06
SCALE = 2.0**-12
AXES = ("gx", "gy", "gz")
BF16 = jnp.bfloat16
F32 = jnp.float32
VMEM = pltpu.VMEM


def ring(array, axis, by):
    n = lax.axis_size(axis)
    return lax.ppermute(array, axis, [(i, (i + by) % n) for i in range(n)])


def sends(face_sums):
    got = [None] * 6
    for dim in (1, 2, 0):
        got[2 * dim + 1] = ring(face_sums[2 * dim], AXES[dim], -1)
        got[2 * dim] = ring(face_sums[2 * dim + 1], AXES[dim], 1)
    return got


def split(x):
    high = x.astype(BF16)
    low = (x - high.astype(F32)).astype(BF16)
    return jnp.concatenate([high, low], axis=0)


def joined(x):
    rows = x.shape[0] // 2
    return x[:rows] + x[rows:]


def put_faces(products, picks, own_ref, face_refs):
    width = picks.shape[2]
    owned = picks.shape[1]
    own_ref[...] = products[:, :owned]
    for face in range(6):
        block = products[:, owned + face * width : owned + (face + 1) * width]
        face_refs[face][...] = joined(
            lax.dot_general(
                split(block),
                picks[face],
                (((1,), (1,)), ((), ())),
                preferred_element_type=F32,
            )
        )


def first_kernel(vector_ref, maps_ref, restricted_ref, picks_ref, own_ref, *face_refs):
    owned = vector_ref.shape[1]
    width = maps_ref.shape[1]
    place = lax.broadcasted_iota(jnp.int32, (owned, width), 0)
    for face in range(6):
        chosen = maps_ref[face : face + 1, :] == place
        picks_ref[face] = jnp.where(chosen, 1.0, 0.0).astype(BF16)
    products = joined(
        jnp.dot(split(vector_ref[...]), restricted_ref[...], preferred_element_type=F32)
    )
    put_faces(products, picks_ref, own_ref, face_refs)


def operator_kernel(*refs):
    vector_ref, got, (picks_ref, schur_ref, own_ref), face_refs = (
        refs[0],
        refs[1:7],
        refs[7:10],
        refs[10:],
    )
    parts = [split(vector_ref[...])]
    for face in range(6):
        parts.append(
            jnp.dot(split(got[face][...]), picks_ref[face], preferred_element_type=F32).astype(BF16)
        )
    products = joined(
        jnp.dot(jnp.concatenate(parts, axis=1), schur_ref[...], preferred_element_type=F32)
    )
    put_faces(products, picks_ref, own_ref, face_refs)


def gram_entries(basis):
    rows = basis[0].shape[0]
    lane = lax.broadcasted_iota(jnp.int32, (rows, 128), 1)
    total = jnp.zeros((rows, 128), F32)
    newest = len(basis) - 1
    for i, vector in enumerate(basis):
        value = jnp.sum(vector * basis[newest], axis=1, keepdims=True)
        total = total + jnp.where(lane == i * 4 + newest, value, 0.0)
    return total


def summed(own_ref, got):
    total = own_ref[...]
    for part in got:
        total = total + part[...]
    return total


def next_kernel(count, *refs):
    own, got, rest = refs[0], refs[1:7], refs[7:]
    older, rest = rest[:count], rest[count:]
    picks_ref, restricted_ref, vector_ref, own_ref = rest[:4]
    face_refs = rest[4:]
    vector = summed(own, got) * SCALE
    vector_ref[...] = vector
    products = joined(jnp.dot(split(vector), restricted_ref[...], preferred_element_type=F32))
    put_faces(products, picks_ref, own_ref, face_refs)


def gram_kernel(*refs):
    own, got = refs[0], refs[1:7]
    older, gram_ref = refs[7:-1], refs[-1]
    basis = [ref[...] for ref in older] + [summed(own, got) * SCALE]
    total = gram_entries(basis[:1])
    for newest in range(1, len(basis)):
        total = total + gram_entries(basis[: newest + 1])
    gram_ref[...] = total


def rotate_solve(columns, beta_norm):
    num_cols = len(columns)
    rhs_vec = [beta_norm] + [jnp.zeros_like(beta_norm) for unused in range(num_cols)]
    cosines = []
    sines = []
    triangle = []
    for section in range(num_cols):
        column = [columns[section][row_at] for row_at in range(section + 2)]
        for earlier in range(section):
            rotated_a = cosines[earlier] * column[earlier] + sines[earlier] * column[earlier + 1]
            rotated_b = -sines[earlier] * column[earlier] + cosines[earlier] * column[earlier + 1]
            column[earlier] = rotated_a
            column[earlier + 1] = rotated_b
        radius = jnp.sqrt(
            column[section] * column[section] + column[section + 1] * column[section + 1]
        )
        cosine = column[section] / radius
        sine_val = column[section + 1] / radius
        column[section] = radius
        cosines.append(cosine)
        sines.append(sine_val)
        rhs_vec[section + 1] = -sine_val * rhs_vec[section]
        rhs_vec[section] = cosine * rhs_vec[section]
        triangle.append(column[: section + 1])
    coeffs = [None] * num_cols
    for section in reversed(range(num_cols)):
        running = rhs_vec[section]
        for onward in range(section + 1, num_cols):
            running = running - triangle[onward][section] * coeffs[onward]
        coeffs[section] = running / triangle[section][section]
    return (coeffs, jnp.abs(rhs_vec[num_cols]))


def combine(gram):
    beta = jnp.sqrt(gram(0, 0) + EPSILON)
    made_of = [[1.0 / beta]]
    columns = []
    for k in range(ITERS):
        applied = [None] + [c * (1.0 / SCALE) for c in made_of[k]]
        against = [
            functools.reduce(
                jnp.add, [gram(a, b) * applied[b] for b in range(1, k + 2)]
            )
            for a in range(k + 1)
        ]
        heights = [
            functools.reduce(jnp.add, [made_of[j][a] * against[a] for a in range(j + 1)])
            for j in range(k + 1)
        ]
        rest = [jnp.zeros_like(beta)] + applied[1:]
        for j in range(k + 1):
            for a in range(j + 1):
                rest[a] = rest[a] - heights[j] * made_of[j][a]
        square = jnp.zeros_like(beta)
        for a in range(k + 2):
            square = square + rest[a] * functools.reduce(
                jnp.add, [gram(a, b) * rest[b] for b in range(k + 2)]
            )
        height = jnp.sqrt(jnp.maximum(square, 0.0) + EPSILON)
        columns.append(heights + [height])
        made_of.append([r / height for r in rest])
    weights, remainder = rotate_solve(columns, beta)
    shares = [
        functools.reduce(jnp.add, [weights[k] * made_of[k][i] for k in range(i, ITERS)])
        for i in range(ITERS)
    ]
    return shares, remainder / beta


def last_kernel(*refs):
    gram_ref, directions = refs[0], refs[1:-2]
    adjoint_ref, ratio_ref = refs[-2:]
    sums = gram_ref[...]

    def gram(a, b):
        at = min(a, b) * 4 + max(a, b)
        return sums[:, at : at + 1]

    shares, ratio = combine(gram)
    total = shares[0] * directions[0][...]
    for i in range(1, ITERS):
        total = total + shares[i] * directions[i][...]
    adjoint_ref[...] = total
    ratio_ref[...] = jnp.broadcast_to(ratio, ratio_ref.shape)


def call(kernel, operands, outputs, name, flops=0, limit=16 << 20):
    bytes_moved = sum(x.size * x.dtype.itemsize for x in operands)
    return pl.pallas_call(
        kernel,
        out_shape=tuple(VMEM(shape, dtype) for shape, dtype in outputs),
        in_specs=[pl.BlockSpec(memory_space=VMEM)] * len(operands),
        out_specs=tuple(pl.BlockSpec(memory_space=VMEM) for _ in outputs),
        compiler_params=pltpu.CompilerParams(vmem_limit_bytes=limit),
        cost_estimate=pl.CostEstimate(flops=flops, bytes_accessed=bytes_moved, transcendentals=0),
        name=name,
    )(*[pltpu.with_memory_space_constraint(x, VMEM) for x in operands])


def all_sum(array, stages):
    for axis in stages:
        n = lax.axis_size(axis)
        spread = jnp.broadcast_to(array[None], (n,) + array.shape)
        array = jnp.sum(lax.all_to_all(spread, axis, 0, 0), axis=0)
    return array


def local(gradient, local_schur, inverse_rows, face_maps):
    vector = gradient[0, 0, 0]
    schur = local_schur[0, 0, 0]
    restricted = inverse_rows[0, 0, 0]
    rows, owned = vector.shape
    width = face_maps.shape[-1]
    exists = []
    for axis in AXES:
        at = lax.axis_index(axis)
        exists += [at > 0, at < lax.axis_size(axis) - 1]
    maps = jnp.where(jnp.stack(exists)[:, None], face_maps[0, 0, 0], -1)

    block = ((rows, owned), F32)
    picks, own, *faces = call(
        first_kernel,
        (vector, maps, restricted),
        (((6, owned, width), BF16),) + (block,) * 7,
        "first",
    )
    basis = [vector]
    directions = []
    for section in range(ITERS):
        got = sends(faces)
        direction = own
        for part in got:
            direction = direction + part
        directions.append(direction)
        got = sends([direction] * 6)
        own, *faces = call(
            operator_kernel, (direction, *got, picks, schur), (block,) * 7, "operator"
        )
        got = sends(faces)
        if section + 1 < ITERS:
            vector, own, *faces = call(
                functools.partial(next_kernel, 0),
                (own, *got, picks, restricted),
                (block,) * 8,
                "next",
            )
            basis.append(vector)
    (gram,) = call(gram_kernel, (own, *got, *basis), (((rows, 128), F32),), "gram")
    gram = all_sum(gram, (("gx", "gy"), "gz"))
    adjoint, ratio = call(
        last_kernel, (gram, *directions), (block, ((rows, 128), F32)), "last"
    )
    return (adjoint[None, None, None], ratio[:, 0])


def solution(mesh):
    placed = P("gx", "gy", "gz", None, None)
    return jax.shard_map(
        local,
        mesh=mesh,
        in_specs=(placed,) * 4,
        out_specs=(placed, P()),
        check_vma=False,
    )
```

```python
import functools

import jax
import jax.numpy as jnp
from jax import lax
from jax.experimental import pallas as pl
from jax.experimental.pallas import tpu as pltpu
from jax.sharding import PartitionSpec as P

ITERS = 3
EPSILON = 1e-06
SCALE = 2.0**-12
AXES = ("gx", "gy", "gz")
EARLY = (0, 1, 2, 3)
LATE = (4, 5)
HOLD = True
BF16 = jnp.bfloat16
F32 = jnp.float32
VMEM = pltpu.VMEM


def swap(array, axis, start):
    n = lax.axis_size(axis)
    pairs = []
    for i in range(start, n + start, 2):
        pairs += [(i % n, (i + 1) % n), ((i + 1) % n, i % n)]
    return lax.ppermute(array, axis, sorted(pairs))


def trade(slots):
    return [swap(slots[slot], AXES[slot // 2], slot % 2) for slot in range(6)]


def even_at(dim):
    return lax.rem(lax.axis_index(AXES[dim]), 2) == 0


def face_of(slot):
    dim = slot // 2
    upper = even_at(dim) if slot % 2 == 0 else jnp.logical_not(even_at(dim))
    return 2 * dim + upper.astype(jnp.int32)


def split(x):
    high = x.astype(BF16)
    low = (x - high.astype(F32)).astype(BF16)
    return jnp.concatenate([high, low], axis=0)


def joined(x):
    rows = x.shape[0] // 2
    return x[:rows] + x[rows:]


def put_faces(products, picks, own_ref, slot_refs):
    width = picks.shape[2]
    owned = picks.shape[1]
    own_ref[...] = products[:, :owned]
    placed = []
    for face in range(6):
        block = products[:, owned + face * width : owned + (face + 1) * width]
        placed.append(
            joined(
                lax.dot_general(
                    split(block),
                    picks[face],
                    (((1,), (1,)), ((), ())),
                    preferred_element_type=F32,
                )
            )
        )
    for dim in range(3):
        even = even_at(dim)
        lower, upper = placed[2 * dim], placed[2 * dim + 1]
        slot_refs[2 * dim][...] = jnp.where(even, upper, lower)
        slot_refs[2 * dim + 1][...] = jnp.where(even, lower, upper)


def first_kernel(*refs):
    sources, outputs, scratch = refs[:3], refs[3:11], refs[11:]
    picks_ref, own_ref, slot_refs = outputs[0], outputs[1], outputs[2:]
    maps_ref, vector_ref, restricted_ref, sems = scratch
    copies = [
        pltpu.make_async_copy(source, target, sems.at[i])
        for i, (source, target) in enumerate(zip(sources, scratch[:3]))
    ]
    for copy in copies:
        copy.start()
    owned = vector_ref.shape[1]
    width = maps_ref.shape[2]
    place = lax.broadcasted_iota(jnp.int32, (owned, width), 0)
    copies[0].wait()
    for dim, axis in enumerate(AXES):
        at = lax.axis_index(axis)
        for side, exists in ((0, at > 0), (1, at < lax.axis_size(axis) - 1)):
            face = 2 * dim + side
            wanted = jnp.where(exists, maps_ref[face], -1)
            picks_ref[face] = jnp.where(wanted == place, 1.0, 0.0).astype(BF16)
    copies[1].wait()
    vector = split(vector_ref[...])
    copies[2].wait()
    products = joined(jnp.dot(vector, restricted_ref[...], preferred_element_type=F32))
    put_faces(products, picks_ref, own_ref, slot_refs)


def hold_kernel(own_ref, schur_ref, out_ref):
    out_ref[...] = own_ref[...]


def own_rows_kernel(vector_ref, schur_ref, total_ref):
    owned = vector_ref.shape[1]
    vector = split(vector_ref[...])
    step = schur_ref.shape[1] // 2

    @pl.loop(0, 2)
    def _(i):
        columns = pl.ds(pl.multiple_of(i * step, step), step)
        total_ref[:, columns] = jnp.dot(
            vector, schur_ref[:owned, columns], preferred_element_type=F32
        )


def picked(slots, got, picks_ref):
    owned, width = picks_ref.shape[1:]
    rows, starts = [], []
    for slot, part in zip(slots, got):
        face = face_of(slot)
        rows.append(
            jnp.dot(split(part[...]), picks_ref[face], preferred_element_type=F32).astype(BF16)
        )
        starts.append(pl.multiple_of(owned + face * width, width))
    return rows, starts


def add_rows(total, rows, starts, schur_ref, columns):
    for row, start in zip(rows, starts):
        block = schur_ref[pl.ds(start, row.shape[1]), columns]
        total = total + jnp.dot(row, block, preferred_element_type=F32)
    return total


def some_rows_kernel(slots, *refs):
    got, (sofar_ref, picks_ref, schur_ref, total_ref) = refs[: len(slots)], refs[len(slots) :]
    rows, starts = picked(slots, got, picks_ref)
    step = schur_ref.shape[1] // 4

    @pl.loop(0, 4)
    def _(i):
        columns = pl.ds(pl.multiple_of(i * step, step), step)
        total_ref[:, columns] = add_rows(sofar_ref[:, columns], rows, starts, schur_ref, columns)


def last_rows_kernel(slots, *refs):
    got, rest = refs[: len(slots)], refs[len(slots) :]
    sofar_ref, picks_ref, schur_ref, own_ref = rest[:4]
    rows, starts = picked(slots, got, picks_ref)
    total = add_rows(sofar_ref[...], rows, starts, schur_ref, slice(None))
    put_faces(joined(total), picks_ref, own_ref, rest[4:])


def gram_entries(basis):
    rows = basis[0].shape[0]
    lane = lax.broadcasted_iota(jnp.int32, (rows, 128), 1)
    total = jnp.zeros((rows, 128), F32)
    newest = len(basis) - 1
    for i, vector in enumerate(basis):
        value = jnp.sum(vector * basis[newest], axis=1, keepdims=True)
        total = total + jnp.where(lane == i * 4 + newest, value, 0.0)
    return total


def summed(own_ref, got):
    total = own_ref[...]
    for part in got:
        total = total + part[...]
    return total


def next_kernel(*refs):
    own, got, rest = refs[0], refs[1:7], refs[7:]
    picks_ref, restricted_ref, vector_ref, own_ref = rest[:4]
    face_refs = rest[4:]
    vector = summed(own, got) * SCALE
    vector_ref[...] = vector
    products = joined(jnp.dot(split(vector), restricted_ref[...], preferred_element_type=F32))
    put_faces(products, picks_ref, own_ref, face_refs)


def gram_kernel(*refs):
    own, got = refs[0], refs[1:7]
    older, gram_ref = refs[7:-1], refs[-1]
    basis = [ref[...] for ref in older] + [summed(own, got) * SCALE]
    total = gram_entries(basis[:1])
    for newest in range(1, len(basis)):
        total = total + gram_entries(basis[: newest + 1])
    half = total.shape[0] // 2
    gram_ref[...] = total[:half] + pltpu.roll(total[half:], 64, 1)


def rotate_solve(columns, beta_norm):
    num_cols = len(columns)
    rhs_vec = [beta_norm] + [jnp.zeros_like(beta_norm) for unused in range(num_cols)]
    cosines = []
    sines = []
    triangle = []
    for section in range(num_cols):
        column = [columns[section][row_at] for row_at in range(section + 2)]
        for earlier in range(section):
            rotated_a = cosines[earlier] * column[earlier] + sines[earlier] * column[earlier + 1]
            rotated_b = -sines[earlier] * column[earlier] + cosines[earlier] * column[earlier + 1]
            column[earlier] = rotated_a
            column[earlier + 1] = rotated_b
        radius = jnp.sqrt(
            column[section] * column[section] + column[section + 1] * column[section + 1]
        )
        cosine = column[section] / radius
        sine_val = column[section + 1] / radius
        column[section] = radius
        cosines.append(cosine)
        sines.append(sine_val)
        rhs_vec[section + 1] = -sine_val * rhs_vec[section]
        rhs_vec[section] = cosine * rhs_vec[section]
        triangle.append(column[: section + 1])
    coeffs = [None] * num_cols
    for section in reversed(range(num_cols)):
        running = rhs_vec[section]
        for onward in range(section + 1, num_cols):
            running = running - triangle[onward][section] * coeffs[onward]
        coeffs[section] = running / triangle[section][section]
    return (coeffs, jnp.abs(rhs_vec[num_cols]))


def combine(gram):
    beta = jnp.sqrt(gram(0, 0) + EPSILON)
    made_of = [[1.0 / beta]]
    columns = []
    for k in range(ITERS):
        applied = [None] + [c * (1.0 / SCALE) for c in made_of[k]]
        against = [
            functools.reduce(
                jnp.add, [gram(a, b) * applied[b] for b in range(1, k + 2)]
            )
            for a in range(k + 1)
        ]
        heights = [
            functools.reduce(jnp.add, [made_of[j][a] * against[a] for a in range(j + 1)])
            for j in range(k + 1)
        ]
        rest = [jnp.zeros_like(beta)] + applied[1:]
        for j in range(k + 1):
            for a in range(j + 1):
                rest[a] = rest[a] - heights[j] * made_of[j][a]
        square = jnp.zeros_like(beta)
        for a in range(k + 2):
            square = square + rest[a] * functools.reduce(
                jnp.add, [gram(a, b) * rest[b] for b in range(k + 2)]
            )
        height = jnp.sqrt(jnp.maximum(square, 0.0) + EPSILON)
        columns.append(heights + [height])
        made_of.append([r / height for r in rest])
    weights, remainder = rotate_solve(columns, beta)
    shares = [
        functools.reduce(jnp.add, [weights[k] * made_of[k][i] for k in range(i, ITERS)])
        for i in range(ITERS)
    ]
    return shares, remainder / beta


def last_kernel(*refs):
    gram_ref, directions = refs[0], refs[1:-2]
    adjoint_ref, ratio_ref = refs[-2:]
    packed = gram_ref[...]
    sums = jnp.concatenate([packed, pltpu.roll(packed, 64, 1)], axis=0)

    def gram(a, b):
        at = min(a, b) * 4 + max(a, b)
        return sums[:, at : at + 1]

    shares, ratio = combine(gram)
    total = shares[0] * directions[0][...]
    for i in range(1, ITERS):
        total = total + shares[i] * directions[i][...]
    adjoint_ref[...] = total
    rows = ratio.shape[0]
    here = lax.broadcasted_iota(jnp.int32, (rows, rows), 0)
    there = lax.broadcasted_iota(jnp.int32, (rows, rows), 1)
    ratio_ref[...] = jnp.sum(jnp.where(here == there, ratio, 0.0), axis=0, keepdims=True)


def call(kernel, operands, outputs, name, keep=True, scratch=(), limit=8 << 20):
    space = pltpu.HBM if scratch else VMEM
    make = VMEM if keep else jax.ShapeDtypeStruct
    operands = [pltpu.with_memory_space_constraint(x, space) for x in operands]
    return pl.pallas_call(
        kernel,
        out_shape=tuple(make(shape, dtype) for shape, dtype in outputs),
        in_specs=[pl.BlockSpec(memory_space=space)] * len(operands),
        out_specs=tuple(pl.BlockSpec(memory_space=VMEM) for _ in outputs),
        scratch_shapes=scratch,
        compiler_params=pltpu.CompilerParams(vmem_limit_bytes=limit),
        cost_estimate=pl.CostEstimate(
            flops=0,
            bytes_accessed=sum(x.size * x.dtype.itemsize for x in operands),
            transcendentals=0,
        ),
        name=name,
    )(*operands)


def all_sum(array, stages):
    for axis in stages:
        n = lax.axis_size(axis)
        spread = jnp.broadcast_to(array[None], (n,) + array.shape)
        array = jnp.sum(lax.all_to_all(spread, axis, 0, 0), axis=0)
    return array


def local(gradient, local_schur, inverse_rows, face_maps):
    vector = gradient[0, 0, 0]
    schur = local_schur[0, 0, 0]
    restricted = inverse_rows[0, 0, 0]
    rows, owned = vector.shape
    width = face_maps.shape[-1]
    maps = face_maps.reshape(6, 1, width)

    block = ((rows, owned), F32)
    wide = ((2 * rows, schur.shape[1]), F32)
    picks, own, *slots = call(
        first_kernel,
        (maps, vector, restricted),
        (((6, owned, width), BF16),) + (block,) * 7,
        "first",
        scratch=[
            VMEM(maps.shape, maps.dtype),
            VMEM(vector.shape, vector.dtype),
            VMEM(restricted.shape, restricted.dtype),
            pltpu.SemaphoreType.DMA((3,)),
        ],
    )
    basis = [vector]
    directions = []
    for section in range(ITERS):
        if section == 0 and HOLD:
            (own,) = call(hold_kernel, (own, schur), (block,), "hold")
        got = trade(slots)
        direction = own
        for part in got:
            direction = direction + part
        directions.append(direction)
        got = trade([direction] * 6)
        (total,) = call(own_rows_kernel, (direction, schur), (wide,), "own_rows")
        (total,) = call(
            functools.partial(some_rows_kernel, EARLY),
            (*[got[slot] for slot in EARLY], total, picks, schur),
            (wide,),
            "some_rows",
        )
        own, *slots = call(
            functools.partial(last_rows_kernel, LATE),
            (*[got[slot] for slot in LATE], total, picks, schur),
            (block,) * 7,
            "last_rows",
        )
        got = trade(slots)
        if section + 1 < ITERS:
            vector, own, *slots = call(
                next_kernel, (own, *got, picks, restricted), (block,) * 8, "next"
            )
            basis.append(vector)
    (gram,) = call(gram_kernel, (own, *got, *basis), (((rows // 2, 128), F32),), "gram")
    gram = all_sum(gram, (("gx", "gy"), "gz"))
    adjoint, ratio = call(
        last_kernel, (gram, *directions), (block, ((1, rows), F32)), "last", keep=False
    )
    return (adjoint[None, None, None], ratio.reshape(rows))


def solution(mesh):
    placed = P("gx", "gy", "gz", None, None)
    return jax.shard_map(
        local,
        mesh=mesh,
        in_specs=(placed,) * 4,
        out_specs=(placed, P()),
        check_vma=False,
    )
```

```python
import functools

import jax
import jax.numpy as jnp
import numpy as np
from jax import lax
from jax.experimental import pallas as pl
from jax.experimental.pallas import tpu as pltpu
from jax.sharding import PartitionSpec as P

ITERS = 3
EPSILON = 1e-06
SCALE = 2.0**-12
AXES = ("gx", "gy", "gz")
ASIDE = (1, 2, 1)
ORDER = (4, 5, 0, 1, 3, 2)
EARLY = ORDER[:4]
LATE = ORDER[4:]
HOLD = True
BF16 = jnp.bfloat16
F32 = jnp.float32
VMEM = pltpu.VMEM


def partners(slot):
    dim = slot // 2
    sizes = [lax.axis_size(axis) for axis in AXES]
    pairs = []
    for place in np.ndindex(*sizes):
        at = list(place)
        step = 1 if (at[dim] - slot) % 2 == 0 else -1
        if 0 <= at[dim] + step < sizes[dim]:
            at[dim] += step
        else:
            beside = ASIDE[dim]
            at[beside] += 1 - 2 * (at[beside] % 2)
        pairs.append(
            tuple(int(np.ravel_multi_index(position, sizes)) for position in (place, at))
        )
    return pairs


def trade(slots):
    return [lax.ppermute(slots[slot], AXES, partners(slot)) for slot in range(6)]


def even_at(dim):
    return lax.rem(lax.axis_index(AXES[dim]), 2) == 0


def face_of(slot):
    dim = slot // 2
    upper = even_at(dim) if slot % 2 == 0 else jnp.logical_not(even_at(dim))
    return 2 * dim + upper.astype(jnp.int32)


def split(x):
    high = x.astype(BF16)
    low = (x - high.astype(F32)).astype(BF16)
    return jnp.concatenate([high, low], axis=0)


def joined(x):
    rows = x.shape[0] // 2
    return x[:rows] + x[rows:]


def put_faces(products, picks, own_ref, slot_refs):
    width = picks.shape[2]
    owned = picks.shape[1]
    own_ref[...] = products[:, :owned]
    placed = []
    for face in range(6):
        block = products[:, owned + face * width : owned + (face + 1) * width]
        placed.append(
            joined(
                lax.dot_general(
                    split(block),
                    picks[face],
                    (((1,), (1,)), ((), ())),
                    preferred_element_type=F32,
                )
            )
        )
    for dim in range(3):
        even = even_at(dim)
        lower, upper = placed[2 * dim], placed[2 * dim + 1]
        slot_refs[2 * dim][...] = jnp.where(even, upper, lower)
        slot_refs[2 * dim + 1][...] = jnp.where(even, lower, upper)


def first_kernel(*refs):
    sources, outputs, scratch = refs[:3], refs[3:11], refs[11:]
    picks_ref, own_ref, slot_refs = outputs[0], outputs[1], outputs[2:]
    maps_ref, vector_ref, restricted_ref, sems = scratch
    copies = [
        pltpu.make_async_copy(source, target, sems.at[i])
        for i, (source, target) in enumerate(zip(sources, scratch[:3]))
    ]
    for copy in copies:
        copy.start()
    owned = vector_ref.shape[1]
    width = maps_ref.shape[2]
    place = lax.broadcasted_iota(jnp.int32, (owned, width), 0)
    copies[0].wait()
    for dim, axis in enumerate(AXES):
        at = lax.axis_index(axis)
        for side, exists in ((0, at > 0), (1, at < lax.axis_size(axis) - 1)):
            face = 2 * dim + side
            wanted = jnp.where(exists, maps_ref[face], -1)
            picks_ref[face] = jnp.where(wanted == place, 1.0, 0.0).astype(BF16)
    copies[1].wait()
    vector = split(vector_ref[...])
    copies[2].wait()
    products = joined(jnp.dot(vector, restricted_ref[...], preferred_element_type=F32))
    put_faces(products, picks_ref, own_ref, slot_refs)


def hold_kernel(own_ref, schur_ref, out_ref):
    out_ref[...] = own_ref[...]


def own_rows_kernel(vector_ref, schur_ref, total_ref):
    owned = vector_ref.shape[1]
    vector = split(vector_ref[...])
    step = schur_ref.shape[1] // 2

    @pl.loop(0, 2)
    def _(i):
        columns = pl.ds(pl.multiple_of(i * step, step), step)
        total_ref[:, columns] = jnp.dot(
            vector, schur_ref[:owned, columns], preferred_element_type=F32
        )


def picked(slots, got, picks_ref):
    owned, width = picks_ref.shape[1:]
    rows, starts = [], []
    for slot, part in zip(slots, got):
        face = face_of(slot)
        rows.append(
            jnp.dot(split(part[...]), picks_ref[face], preferred_element_type=F32).astype(BF16)
        )
        starts.append(pl.multiple_of(owned + face * width, width))
    return rows, starts


def add_rows(total, rows, starts, schur_ref, columns):
    for row, start in zip(rows, starts):
        block = schur_ref[pl.ds(start, row.shape[1]), columns]
        total = total + jnp.dot(row, block, preferred_element_type=F32)
    return total


def some_rows_kernel(slots, *refs):
    got, (sofar_ref, picks_ref, schur_ref, total_ref) = refs[: len(slots)], refs[len(slots) :]
    rows, starts = picked(slots, got, picks_ref)
    step = schur_ref.shape[1] // 4

    @pl.loop(0, 4)
    def _(i):
        columns = pl.ds(pl.multiple_of(i * step, step), step)
        total_ref[:, columns] = add_rows(sofar_ref[:, columns], rows, starts, schur_ref, columns)


def last_rows_kernel(slots, *refs):
    got, rest = refs[: len(slots)], refs[len(slots) :]
    sofar_ref, picks_ref, schur_ref, own_ref = rest[:4]
    rows, starts = picked(slots, got, picks_ref)
    total = add_rows(sofar_ref[...], rows, starts, schur_ref, slice(None))
    put_faces(joined(total), picks_ref, own_ref, rest[4:])


def gram_entries(basis):
    rows = basis[0].shape[0]
    lane = lax.broadcasted_iota(jnp.int32, (rows, 128), 1)
    total = jnp.zeros((rows, 128), F32)
    newest = len(basis) - 1
    for i, vector in enumerate(basis):
        value = jnp.sum(vector * basis[newest], axis=1, keepdims=True)
        total = total + jnp.where(lane == i * 4 + newest, value, 0.0)
    return total


def summed(own_ref, got):
    total = own_ref[...]
    for part in got:
        total = total + part[...]
    return total


def next_kernel(*refs):
    own, got, rest = refs[0], refs[1:7], refs[7:]
    picks_ref, restricted_ref, vector_ref, own_ref = rest[:4]
    face_refs = rest[4:]
    vector = summed(own, got) * SCALE
    vector_ref[...] = vector
    products = joined(jnp.dot(split(vector), restricted_ref[...], preferred_element_type=F32))
    put_faces(products, picks_ref, own_ref, face_refs)


def gram_kernel(*refs):
    own, got = refs[0], refs[1:7]
    older, gram_ref = refs[7:-1], refs[-1]
    basis = [ref[...] for ref in older] + [summed(own, got) * SCALE]
    total = gram_entries(basis[:1])
    for newest in range(1, len(basis)):
        total = total + gram_entries(basis[: newest + 1])
    half = total.shape[0] // 2
    gram_ref[...] = total[:half] + pltpu.roll(total[half:], 64, 1)


def rotate_solve(columns, beta_norm):
    num_cols = len(columns)
    rhs_vec = [beta_norm] + [jnp.zeros_like(beta_norm) for unused in range(num_cols)]
    cosines = []
    sines = []
    triangle = []
    for section in range(num_cols):
        column = [columns[section][row_at] for row_at in range(section + 2)]
        for earlier in range(section):
            rotated_a = cosines[earlier] * column[earlier] + sines[earlier] * column[earlier + 1]
            rotated_b = -sines[earlier] * column[earlier] + cosines[earlier] * column[earlier + 1]
            column[earlier] = rotated_a
            column[earlier + 1] = rotated_b
        radius = jnp.sqrt(
            column[section] * column[section] + column[section + 1] * column[section + 1]
        )
        cosine = column[section] / radius
        sine_val = column[section + 1] / radius
        column[section] = radius
        cosines.append(cosine)
        sines.append(sine_val)
        rhs_vec[section + 1] = -sine_val * rhs_vec[section]
        rhs_vec[section] = cosine * rhs_vec[section]
        triangle.append(column[: section + 1])
    coeffs = [None] * num_cols
    for section in reversed(range(num_cols)):
        running = rhs_vec[section]
        for onward in range(section + 1, num_cols):
            running = running - triangle[onward][section] * coeffs[onward]
        coeffs[section] = running / triangle[section][section]
    return (coeffs, jnp.abs(rhs_vec[num_cols]))


def combine(gram):
    beta = jnp.sqrt(gram(0, 0) + EPSILON)
    made_of = [[1.0 / beta]]
    columns = []
    for k in range(ITERS):
        applied = [None] + [c * (1.0 / SCALE) for c in made_of[k]]
        against = [
            functools.reduce(
                jnp.add, [gram(a, b) * applied[b] for b in range(1, k + 2)]
            )
            for a in range(k + 1)
        ]
        heights = [
            functools.reduce(jnp.add, [made_of[j][a] * against[a] for a in range(j + 1)])
            for j in range(k + 1)
        ]
        rest = [jnp.zeros_like(beta)] + applied[1:]
        for j in range(k + 1):
            for a in range(j + 1):
                rest[a] = rest[a] - heights[j] * made_of[j][a]
        square = jnp.zeros_like(beta)
        for a in range(k + 2):
            square = square + rest[a] * functools.reduce(
                jnp.add, [gram(a, b) * rest[b] for b in range(k + 2)]
            )
        height = jnp.sqrt(jnp.maximum(square, 0.0) + EPSILON)
        columns.append(heights + [height])
        made_of.append([r / height for r in rest])
    weights, remainder = rotate_solve(columns, beta)
    shares = [
        functools.reduce(jnp.add, [weights[k] * made_of[k][i] for k in range(i, ITERS)])
        for i in range(ITERS)
    ]
    return shares, remainder / beta


def last_kernel(*refs):
    gram_ref, directions = refs[0], refs[1:-2]
    adjoint_ref, ratio_ref = refs[-2:]
    packed = gram_ref[...]
    sums = jnp.concatenate([packed, pltpu.roll(packed, 64, 1)], axis=0)

    def gram(a, b):
        at = min(a, b) * 4 + max(a, b)
        return sums[:, at : at + 1]

    shares, ratio = combine(gram)
    total = shares[0] * directions[0][...]
    for i in range(1, ITERS):
        total = total + shares[i] * directions[i][...]
    adjoint_ref[...] = total
    rows = ratio.shape[0]
    here = lax.broadcasted_iota(jnp.int32, (rows, rows), 0)
    there = lax.broadcasted_iota(jnp.int32, (rows, rows), 1)
    ratio_ref[...] = jnp.sum(jnp.where(here == there, ratio, 0.0), axis=0, keepdims=True)


def call(kernel, operands, outputs, name, keep=True, scratch=(), limit=8 << 20):
    space = pltpu.HBM if scratch else VMEM
    make = VMEM if keep else jax.ShapeDtypeStruct
    operands = [pltpu.with_memory_space_constraint(x, space) for x in operands]
    return pl.pallas_call(
        kernel,
        out_shape=tuple(make(shape, dtype) for shape, dtype in outputs),
        in_specs=[pl.BlockSpec(memory_space=space)] * len(operands),
        out_specs=tuple(pl.BlockSpec(memory_space=VMEM) for _ in outputs),
        scratch_shapes=scratch,
        compiler_params=pltpu.CompilerParams(vmem_limit_bytes=limit),
        cost_estimate=pl.CostEstimate(
            flops=0,
            bytes_accessed=sum(x.size * x.dtype.itemsize for x in operands),
            transcendentals=0,
        ),
        name=name,
    )(*operands)


def all_sum(array, stages):
    for axis in stages:
        n = lax.axis_size(axis)
        spread = jnp.broadcast_to(array[None], (n,) + array.shape)
        array = jnp.sum(lax.all_to_all(spread, axis, 0, 0), axis=0)
    return array


def local(gradient, local_schur, inverse_rows, face_maps):
    vector = gradient[0, 0, 0]
    schur = local_schur[0, 0, 0]
    restricted = inverse_rows[0, 0, 0]
    rows, owned = vector.shape
    width = face_maps.shape[-1]
    maps = face_maps.reshape(6, 1, width)

    block = ((rows, owned), F32)
    wide = ((2 * rows, schur.shape[1]), F32)
    picks, own, *slots = call(
        first_kernel,
        (maps, vector, restricted),
        (((6, owned, width), BF16),) + (block,) * 7,
        "first",
        scratch=[
            VMEM(maps.shape, maps.dtype),
            VMEM(vector.shape, vector.dtype),
            VMEM(restricted.shape, restricted.dtype),
            pltpu.SemaphoreType.DMA((3,)),
        ],
    )
    basis = [vector]
    directions = []
    for section in range(ITERS):
        if section == 0 and HOLD:
            (own,) = call(hold_kernel, (own, schur), (block,), "hold")
        got = trade(slots)
        direction = own
        for slot in ORDER:
            direction = direction + got[slot]
        directions.append(direction)
        got = trade([direction] * 6)
        (total,) = call(own_rows_kernel, (direction, schur), (wide,), "own_rows")
        (total,) = call(
            functools.partial(some_rows_kernel, EARLY),
            (*[got[slot] for slot in EARLY], total, picks, schur),
            (wide,),
            "some_rows",
        )
        own, *slots = call(
            functools.partial(last_rows_kernel, LATE),
            (*[got[slot] for slot in LATE], total, picks, schur),
            (block,) * 7,
            "last_rows",
        )
        got = trade(slots)
        if section + 1 < ITERS:
            vector, own, *slots = call(
                next_kernel,
                (own, *[got[slot] for slot in ORDER], picks, restricted),
                (block,) * 8,
                "next",
            )
            basis.append(vector)
    (gram,) = call(gram_kernel, (own, *[got[slot] for slot in ORDER], *basis), (((rows // 2, 128), F32),), "gram")
    gram = all_sum(gram, (("gx", "gy"), "gz"))
    adjoint, ratio = call(
        last_kernel, (gram, *directions), (block, ((1, rows), F32)), "last", keep=False
    )
    return (adjoint[None, None, None], ratio.reshape(rows))


def solution(mesh):
    placed = P("gx", "gy", "gz", None, None)
    return jax.shard_map(
        local,
        mesh=mesh,
        in_specs=(placed,) * 4,
        out_specs=(placed, P()),
        check_vma=False,
    )
```

```python
import functools

import jax
import jax.numpy as jnp
import numpy as np
from jax import lax
from jax.experimental import pallas as pl
from jax.experimental.pallas import tpu as pltpu
from jax.sharding import PartitionSpec as P

ITERS = 3
EPSILON = 1e-06
SCALE = 2.0**-12
AXES = ("gx", "gy", "gz")
ASIDE = (1, 2, 1)
ORDER = (4, 5, 0, 1, 3, 2)
EARLY = (2, 0)
LATE = 1
BF16 = jnp.bfloat16
F32 = jnp.float32
VMEM = pltpu.VMEM


def partners(slot):
    dim = slot // 2
    sizes = [lax.axis_size(axis) for axis in AXES]
    pairs = []
    for place in np.ndindex(*sizes):
        at = list(place)
        step = 1 if (at[dim] - slot) % 2 == 0 else -1
        if 0 <= at[dim] + step < sizes[dim]:
            at[dim] += step
        else:
            beside = ASIDE[dim]
            at[beside] += 1 - 2 * (at[beside] % 2)
        pairs.append(
            tuple(int(np.ravel_multi_index(position, sizes)) for position in (place, at))
        )
    return pairs


def trade(slots):
    return [lax.ppermute(slots[slot], AXES, partners(slot)) for slot in range(6)]


def even_at(dim):
    return lax.rem(lax.axis_index(AXES[dim]), 2) == 0


def sides_of(pair, dim):
    even, odd = pair
    here = even_at(dim)
    return jnp.where(here, odd, even), jnp.where(here, even, odd)


def meets(slot):
    at = lax.axis_index(AXES[slot // 2])
    if slot % 2 == 0:
        return at >= 0
    return jnp.logical_and(at > 0, at < lax.axis_size(AXES[slot // 2]) - 1)


def split(x):
    high = x.astype(BF16)
    low = (x - high.astype(F32)).astype(BF16)
    return jnp.concatenate([high, low], axis=0)


def joined(x):
    rows = x.shape[0] // 2
    return x[:rows] + x[rows:]


def ordered(got):
    return [got[slot] for slot in ORDER]


def slot_order(got):
    return [got[ORDER.index(slot)] for slot in range(6)]


def by_slot(products):
    width = products.shape[1] // 6
    blocks = [products[:, face * width : (face + 1) * width] for face in range(6)]
    slots = []
    for dim in range(3):
        slots += sides_of((blocks[2 * dim], blocks[2 * dim + 1]), dim)
    return slots


def put_split(slots, refs):
    for block, ref in zip(slots, refs):
        ref[...] = split(block)


def first_kernel(*refs):
    sources, own_ref, slot_refs, scratch = refs[:3], refs[3], refs[4:10], refs[10:]
    maps_ref, vector_ref, restricted_ref, sems = scratch
    copies = [
        pltpu.make_async_copy(source, target, sems.at[i])
        for i, (source, target) in enumerate(zip(sources, scratch[:3]))
    ]
    for copy in copies:
        copy.start()
    for copy in copies:
        copy.wait()
    rows, owned = vector_ref.shape
    products = joined(
        jnp.dot(split(vector_ref[...]), restricted_ref[...], preferred_element_type=F32)
    )
    own_ref[...] = products[:, :owned]
    maps = jnp.concatenate([maps_ref[face].astype(F32) for face in range(6)], axis=1)
    maps = jnp.broadcast_to(maps, (8, maps.shape[1]))
    for block, row, ref in zip(by_slot(products[:, owned:]), by_slot(maps), slot_refs):
        ref[:rows] = block
        ref[rows:] = row


def added(slots, got, places_ref):
    width = got[0].shape[1]
    total = None
    for slot, part in zip(slots, got):
        place = places_ref[slot * width : (slot + 1) * width, :]
        product = jnp.dot(part[...], place, preferred_element_type=F32)
        total = product if total is None else total + product
    return joined(total)


def early_kernel(*refs):
    own_ref, got, places_ref, sum_ref = refs[0], refs[1:5], refs[5], refs[6]
    sum_ref[...] = own_ref[...] + added(ORDER[:4], got, places_ref)


def turn_kernel(*refs):
    got, places_ref = refs[:6], refs[7]
    width = got[0].shape[1]
    owned = places_ref.shape[1]
    place = lax.broadcasted_iota(jnp.int32, (width, owned), 1)
    for slot in range(6):
        column = jnp.transpose(got[slot][got[slot].shape[0] - 8 :, :])[:, :1].astype(jnp.int32)
        wanted = jnp.where(meets(slot), column, -1)
        places_ref[slot * width : (slot + 1) * width, :] = jnp.where(
            wanted == place, 1.0, 0.0
        ).astype(BF16)


def offer(vector, picks_ref, slot_refs):
    taken = jnp.dot(split(vector), picks_ref[...], preferred_element_type=F32).astype(BF16)
    width = taken.shape[1] // 6
    for slot in range(6):
        slot_refs[slot][...] = taken[:, slot * width : (slot + 1) * width]


def meet_kernel(*refs):
    own_ref, got, direction_ref, picks_ref = refs[0], slot_order(refs[1:7]), refs[7], refs[8]
    rows, owned = own_ref.shape
    width = got[0].shape[1]
    place = lax.broadcasted_iota(jnp.int32, (owned, width), 0)
    for slot in range(6):
        row = got[slot][rows : rows + 1, :].astype(jnp.int32)
        wanted = jnp.where(meets(slot), row, -1)
        picks_ref[:, slot * width : (slot + 1) * width] = jnp.where(
            wanted == place, 1.0, 0.0
        ).astype(BF16)
    parts = jnp.concatenate([split(ref[:rows]) for ref in got], axis=1)
    direction = own_ref[...] + joined(
        lax.dot_general(
            parts, picks_ref[...], (((1,), (1,)), ((), ())), preferred_element_type=F32
        )
    )
    direction_ref[...] = direction
    offer(direction, picks_ref, refs[9:])


def direction_kernel(*refs):
    sum_ref, got, places_ref, picks_ref, direction_ref = refs[0], refs[1:3], *refs[3:6]
    direction = sum_ref[...] + added(ORDER[4:], got, places_ref)
    direction_ref[...] = direction
    offer(direction, picks_ref, refs[6:])


def hold_kernel(own_ref, schur_ref, out_ref):
    out_ref[...] = own_ref[...]


def own_rows_kernel(vector_ref, schur_ref, total_ref):
    owned = vector_ref.shape[1]
    vector = split(vector_ref[...])
    step = total_ref.shape[1] // 2

    @pl.loop(0, 2)
    def _(i):
        at = pl.multiple_of(i * step, step)
        block = schur_ref[:owned, pl.ds(pl.multiple_of(owned + at, 128), step)]
        total_ref[:, pl.ds(at, step)] = jnp.dot(vector, block, preferred_element_type=F32)


def of_dim(dim, got):
    return jnp.concatenate(sides_of([ref[...] for ref in got], dim), axis=1)


def rows_of(dim, row, owned):
    start = owned + dim * row.shape[1]
    return slice(start, start + row.shape[1])


def some_rows_kernel(*refs):
    got, (sofar_ref, schur_ref, total_ref) = refs[:4], refs[4:]
    wide = total_ref.shape[1]
    owned = schur_ref.shape[1] - wide
    parts = [(dim, of_dim(dim, got[2 * i : 2 * i + 2])) for i, dim in enumerate(EARLY)]
    step = wide // 3

    @pl.loop(0, 3)
    def _(i):
        at = pl.multiple_of(i * step, step)
        columns = pl.ds(pl.multiple_of(owned + at, 128), step)
        here = pl.ds(at, step)
        total = sofar_ref[:, here]
        for dim, row in parts:
            block = schur_ref[rows_of(dim, row, owned), columns]
            total = total + jnp.dot(row, block, preferred_element_type=F32)
        total_ref[:, here] = total


def last_rows_kernel(*refs):
    got, (sofar_ref, schur_ref), slot_refs = refs[:2], refs[2:4], refs[4:]
    owned = schur_ref.shape[1] - sofar_ref.shape[1]
    row = of_dim(LATE, got[::-1])
    block = schur_ref[rows_of(LATE, row, owned), owned:]
    total = sofar_ref[...] + jnp.dot(row, block, preferred_element_type=F32)
    put_split(by_slot(joined(total)), slot_refs)


def own_columns_kernel(*refs):
    vector_ref, got, schur_ref, own_ref = refs[0], slot_order(refs[1:7]), refs[7], refs[8]
    owned = vector_ref.shape[1]
    row = jnp.concatenate(
        [split(vector_ref[...])] + [of_dim(dim, got[2 * dim : 2 * dim + 2]) for dim in range(3)],
        axis=1,
    )
    step = owned // 2

    @pl.loop(0, 2)
    def _(i):
        columns = pl.ds(pl.multiple_of(i * step, step), step)
        own_ref[:, columns] = joined(
            jnp.dot(row, schur_ref[:, columns], preferred_element_type=F32)
        )


def gram_entries(basis):
    rows = basis[0].shape[0]
    lane = lax.broadcasted_iota(jnp.int32, (rows, 128), 1)
    total = jnp.zeros((rows, 128), F32)
    newest = len(basis) - 1
    for i, vector in enumerate(basis):
        value = jnp.sum(vector * basis[newest], axis=1, keepdims=True)
        total = total + jnp.where(lane == i * 4 + newest, value, 0.0)
    return total


def next_kernel(*refs):
    sum_ref, got, places_ref, restricted_ref = refs[0], refs[1:3], refs[3], refs[4]
    vector_ref, next_ref, slot_refs = refs[5], refs[6], refs[7:]
    vector = (sum_ref[...] + added(ORDER[4:], got, places_ref)) * SCALE
    vector_ref[...] = vector
    products = joined(jnp.dot(split(vector), restricted_ref[...], preferred_element_type=F32))
    owned = vector.shape[1]
    next_ref[...] = products[:, :owned]
    put_split(by_slot(products[:, owned:]), slot_refs)


def gram_kernel(*refs):
    sum_ref, got, places_ref = refs[0], refs[1:3], refs[3]
    older, gram_ref = refs[4:-1], refs[-1]
    last = (sum_ref[...] + added(ORDER[4:], got, places_ref)) * SCALE
    basis = [ref[...] for ref in older] + [last]
    total = gram_entries(basis[:1])
    for newest in range(1, len(basis)):
        total = total + gram_entries(basis[: newest + 1])
    half = total.shape[0] // 2
    gram_ref[...] = total[:half] + pltpu.roll(total[half:], 64, 1)


def rotate_solve(columns, beta_norm):
    num_cols = len(columns)
    rhs_vec = [beta_norm] + [jnp.zeros_like(beta_norm) for unused in range(num_cols)]
    cosines = []
    sines = []
    triangle = []
    for section in range(num_cols):
        column = [columns[section][row_at] for row_at in range(section + 2)]
        for earlier in range(section):
            rotated_a = cosines[earlier] * column[earlier] + sines[earlier] * column[earlier + 1]
            rotated_b = -sines[earlier] * column[earlier] + cosines[earlier] * column[earlier + 1]
            column[earlier] = rotated_a
            column[earlier + 1] = rotated_b
        radius = jnp.sqrt(
            column[section] * column[section] + column[section + 1] * column[section + 1]
        )
        inverse = 1.0 / radius
        cosine = column[section] * inverse
        sine_val = column[section + 1] * inverse
        column[section] = inverse
        cosines.append(cosine)
        sines.append(sine_val)
        rhs_vec[section + 1] = -sine_val * rhs_vec[section]
        rhs_vec[section] = cosine * rhs_vec[section]
        triangle.append(column[: section + 1])
    coeffs = [None] * num_cols
    for section in reversed(range(num_cols)):
        running = rhs_vec[section]
        for onward in range(section + 1, num_cols):
            running = running - triangle[onward][section] * coeffs[onward]
        coeffs[section] = running * triangle[section][section]
    return (coeffs, jnp.abs(rhs_vec[num_cols]))


def combine(gram):
    beta = jnp.sqrt(gram(0, 0) + EPSILON)
    inverse_beta = 1.0 / beta
    made_of = [[inverse_beta]]
    columns = []
    for k in range(ITERS):
        applied = [None] + [c * (1.0 / SCALE) for c in made_of[k]]
        against = [
            functools.reduce(
                jnp.add, [gram(a, b) * applied[b] for b in range(1, k + 2)]
            )
            for a in range(k + 1)
        ]
        heights = [
            functools.reduce(jnp.add, [made_of[j][a] * against[a] for a in range(j + 1)])
            for j in range(k + 1)
        ]
        rest = [jnp.zeros_like(beta)] + applied[1:]
        for j in range(k + 1):
            for a in range(j + 1):
                rest[a] = rest[a] - heights[j] * made_of[j][a]
        square = jnp.zeros_like(beta)
        for a in range(k + 2):
            square = square + rest[a] * functools.reduce(
                jnp.add, [gram(a, b) * rest[b] for b in range(k + 2)]
            )
        height = jnp.sqrt(jnp.maximum(square, 0.0) + EPSILON)
        columns.append(heights + [height])
        inverse = 1.0 / height
        made_of.append([r * inverse for r in rest])
    weights, remainder = rotate_solve(columns, beta)
    shares = [
        functools.reduce(jnp.add, [weights[k] * made_of[k][i] for k in range(i, ITERS)])
        for i in range(ITERS)
    ]
    return shares, remainder * inverse_beta


def last_kernel(*refs):
    gram_ref, directions = refs[0], refs[1:-2]
    adjoint_ref, ratio_ref = refs[-2:]
    packed = gram_ref[...]
    sums = jnp.concatenate([packed, pltpu.roll(packed, 64, 1)], axis=0)

    def gram(a, b):
        at = min(a, b) * 4 + max(a, b)
        return sums[:, at : at + 1]

    shares, ratio = combine(gram)
    total = shares[0] * directions[0][...]
    for i in range(1, ITERS):
        total = total + shares[i] * directions[i][...]
    adjoint_ref[...] = total
    rows = ratio.shape[0]
    here = lax.broadcasted_iota(jnp.int32, (rows, rows), 0)
    there = lax.broadcasted_iota(jnp.int32, (rows, rows), 1)
    ratio_ref[...] = jnp.sum(jnp.where(here == there, ratio, 0.0), axis=0, keepdims=True)


def call(kernel, operands, outputs, name, keep=True, scratch=(), limit=8 << 20):
    space = pltpu.HBM if scratch else VMEM
    make = VMEM if keep else jax.ShapeDtypeStruct
    operands = [pltpu.with_memory_space_constraint(x, space) for x in operands]
    return pl.pallas_call(
        kernel,
        out_shape=tuple(make(shape, dtype) for shape, dtype in outputs),
        in_specs=[pl.BlockSpec(memory_space=space)] * len(operands),
        out_specs=tuple(pl.BlockSpec(memory_space=VMEM) for _ in outputs),
        scratch_shapes=scratch,
        compiler_params=pltpu.CompilerParams(vmem_limit_bytes=limit),
        cost_estimate=pl.CostEstimate(
            flops=0,
            bytes_accessed=sum(x.size * x.dtype.itemsize for x in operands),
            transcendentals=0,
        ),
        name=name,
    )(*operands)


def all_sum(array, stages):
    for axis in stages:
        n = lax.axis_size(axis)
        spread = jnp.broadcast_to(array[None], (n,) + array.shape)
        array = jnp.sum(lax.all_to_all(spread, axis, 0, 0), axis=0)
    return array


def local(gradient, local_schur, inverse_rows, face_maps):
    vector = gradient[0, 0, 0]
    schur = local_schur[0, 0, 0]
    restricted = inverse_rows[0, 0, 0]
    rows, owned = vector.shape
    width = face_maps.shape[-1]
    maps = face_maps.reshape(6, 1, width)

    block = ((rows, owned), F32)
    wide = ((2 * rows, 6 * width), F32)
    parcel = ((2 * rows, width), BF16)
    own, *slots = call(
        first_kernel,
        (maps, vector, restricted),
        (block,) + (((rows + 8, width), F32),) * 6,
        "first",
        scratch=[
            VMEM(maps.shape, maps.dtype),
            VMEM(vector.shape, vector.dtype),
            VMEM(restricted.shape, restricted.dtype),
            pltpu.SemaphoreType.DMA((3,)),
        ],
    )
    basis = [vector]
    directions = []
    for section in range(ITERS):
        if section == 0:
            (own,) = call(hold_kernel, (own, schur), (block,), "hold")
        got = trade(slots)
        if section == 0:
            parcels = got
            direction, picks, *slots = call(
                meet_kernel,
                (own, *ordered(got)),
                (block, ((owned, 6 * width), BF16)) + (parcel,) * 6,
                "meet",
            )
        else:
            got = ordered(got)
            (own,) = call(early_kernel, (own, *got[:4], places), (block,), "early")
            direction, *slots = call(
                direction_kernel, (own, *got[4:], places, picks), (block,) + (parcel,) * 6,
                "direction",
            )
        directions.append(direction)
        got = trade(slots)
        (total,) = call(own_rows_kernel, (direction, schur), (wide,), "own_rows")
        early = [got[2 * dim + side] for dim in EARLY for side in range(2)]
        late = [got[2 * LATE + 1], got[2 * LATE]]
        (total,) = call(some_rows_kernel, (*early, total, schur), (wide,), "some_rows")
        slots = call(last_rows_kernel, (*late, total, schur), (parcel,) * 6, "last_rows")
        (own,) = call(
            own_columns_kernel, (direction, *ordered(got), schur), (block,), "own_columns"
        )
        if section == 0:
            (places,) = call(
                turn_kernel, (*parcels, slots[0]), (((6 * width, owned), BF16),), "turn"
            )
        got = ordered(trade(slots))
        (own,) = call(early_kernel, (own, *got[:4], places), (block,), "early")
        if section + 1 < ITERS:
            vector, own, *slots = call(
                next_kernel,
                (own, *got[4:], places, restricted),
                (block,) * 2 + (parcel,) * 6,
                "next",
            )
            basis.append(vector)
    (gram,) = call(
        gram_kernel, (own, *got[4:], places, *basis), (((rows // 2, 128), F32),), "gram"
    )
    gram = all_sum(gram, (("gx", "gy"), "gz"))
    adjoint, ratio = call(
        last_kernel, (gram, *directions), (block, ((1, rows), F32)), "last", keep=False
    )
    return (adjoint[None, None, None], ratio.reshape(rows))


def solution(mesh):
    placed = P("gx", "gy", "gz", None, None)
    return jax.shard_map(
        local,
        mesh=mesh,
        in_specs=(placed,) * 4,
        out_specs=(placed, P()),
        check_vma=False,
    )
```

```python
import functools

import jax
import jax.numpy as jnp
import numpy as np
from jax import lax
from jax.experimental import pallas as pl
from jax.experimental.pallas import tpu as pltpu
from jax.sharding import PartitionSpec as P

ITERS = 3
EPSILON = 1e-06
SCALE = 2.0**-12
AXES = ("gx", "gy", "gz")
ASIDE = (1, 0, 1)
ORDER = (4, 5, 0, 1, 3, 2)
EARLY = (2, 0)
LATE = 1
BF16 = jnp.bfloat16
F32 = jnp.float32
VMEM = pltpu.VMEM


def partners(slot):
    dim = slot // 2
    sizes = [lax.axis_size(axis) for axis in AXES]
    pairs = []
    for place in np.ndindex(*sizes):
        at = list(place)
        step = 1 if (at[dim] - slot) % 2 == 0 else -1
        if 0 <= at[dim] + step < sizes[dim]:
            at[dim] += step
        else:
            beside = ASIDE[dim]
            at[beside] += 1 - 2 * (at[beside] % 2)
        pairs.append(
            tuple(int(np.ravel_multi_index(position, sizes)) for position in (place, at))
        )
    return pairs


def trade(slots):
    return [lax.ppermute(slots[slot], AXES, partners(slot)) for slot in range(6)]


def even_at(dim):
    return lax.rem(lax.axis_index(AXES[dim]), 2) == 0


def sides_of(pair, dim):
    even, odd = pair
    here = even_at(dim)
    return jnp.where(here, odd, even), jnp.where(here, even, odd)


def meets(slot):
    at = lax.axis_index(AXES[slot // 2])
    if slot % 2 == 0:
        return at >= 0
    return jnp.logical_and(at > 0, at < lax.axis_size(AXES[slot // 2]) - 1)


def split(x):
    high = x.astype(BF16)
    low = (x - high.astype(F32)).astype(BF16)
    return jnp.concatenate([high, low], axis=0)


def joined(x):
    rows = x.shape[0] // 2
    return x[:rows] + x[rows:]


def ordered(got):
    return [got[slot] for slot in ORDER]


def slot_order(got):
    return [got[ORDER.index(slot)] for slot in range(6)]


def by_slot(products):
    width = products.shape[1] // 6
    blocks = [products[:, face * width : (face + 1) * width] for face in range(6)]
    slots = []
    for dim in range(3):
        slots += sides_of((blocks[2 * dim], blocks[2 * dim + 1]), dim)
    return slots


def put_split(slots, refs):
    for block, ref in zip(slots, refs):
        ref[...] = split(block)


def first_kernel(*refs):
    sources, own_ref, slot_refs, scratch = refs[:3], refs[3], refs[4:10], refs[10:]
    maps_ref, vector_ref, restricted_ref, sems = scratch
    copies = [
        pltpu.make_async_copy(source, target, sems.at[i])
        for i, (source, target) in enumerate(zip(sources, scratch[:3]))
    ]
    for copy in copies:
        copy.start()
    for copy in copies:
        copy.wait()
    rows, owned = vector_ref.shape
    products = joined(
        jnp.dot(split(vector_ref[...]), restricted_ref[...], preferred_element_type=F32)
    )
    own_ref[...] = products[:, :owned]
    maps = jnp.concatenate([maps_ref[face].astype(F32) for face in range(6)], axis=1)
    maps = jnp.broadcast_to(maps, (8, maps.shape[1]))
    for block, row, ref in zip(by_slot(products[:, owned:]), by_slot(maps), slot_refs):
        ref[:rows] = block
        ref[rows:] = row


def added(slots, got, places_ref):
    width = got[0].shape[1]
    total = None
    for slot, part in zip(slots, got):
        place = places_ref[slot * width : (slot + 1) * width, :]
        product = jnp.dot(part[...], place, preferred_element_type=F32)
        total = product if total is None else total + product
    return joined(total)


def early_kernel(*refs):
    own_ref, got, places_ref, sum_ref = refs[0], refs[1:5], refs[5], refs[6]
    sum_ref[...] = own_ref[...] + added(ORDER[:4], got, places_ref)


def turn_kernel(*refs):
    got, places_ref = refs[:6], refs[7]
    width = got[0].shape[1]
    owned = places_ref.shape[1]
    place = lax.broadcasted_iota(jnp.int32, (width, owned), 1)
    for slot in range(6):
        column = jnp.transpose(got[slot][got[slot].shape[0] - 8 :, :])[:, :1].astype(jnp.int32)
        wanted = jnp.where(meets(slot), column, -1)
        places_ref[slot * width : (slot + 1) * width, :] = jnp.where(
            wanted == place, 1.0, 0.0
        ).astype(BF16)


def offer(vector, picks_ref, slot_refs):
    taken = jnp.dot(split(vector), picks_ref[...], preferred_element_type=F32).astype(BF16)
    width = taken.shape[1] // 6
    for slot in range(6):
        slot_refs[slot][...] = taken[:, slot * width : (slot + 1) * width]


def meet_kernel(*refs):
    own_ref, got, direction_ref, picks_ref = refs[0], slot_order(refs[1:7]), refs[7], refs[8]
    rows, owned = own_ref.shape
    width = got[0].shape[1]
    place = lax.broadcasted_iota(jnp.int32, (owned, width), 0)
    for slot in range(6):
        row = got[slot][rows : rows + 1, :].astype(jnp.int32)
        wanted = jnp.where(meets(slot), row, -1)
        picks_ref[:, slot * width : (slot + 1) * width] = jnp.where(
            wanted == place, 1.0, 0.0
        ).astype(BF16)
    parts = jnp.concatenate([split(ref[:rows]) for ref in got], axis=1)
    direction = own_ref[...] + joined(
        lax.dot_general(
            parts, picks_ref[...], (((1,), (1,)), ((), ())), preferred_element_type=F32
        )
    )
    direction_ref[...] = direction
    offer(direction, picks_ref, refs[9:])


def direction_kernel(*refs):
    sum_ref, got, places_ref, picks_ref, direction_ref = refs[0], refs[1:3], *refs[3:6]
    direction = sum_ref[...] + added(ORDER[4:], got, places_ref)
    direction_ref[...] = direction
    offer(direction, picks_ref, refs[6:])


def hold_kernel(own_ref, schur_ref, out_ref):
    out_ref[...] = own_ref[...]


def own_rows_kernel(vector_ref, schur_ref, total_ref):
    owned = vector_ref.shape[1]
    vector = split(vector_ref[...])
    step = total_ref.shape[1] // 2

    @pl.loop(0, 2)
    def _(i):
        at = pl.multiple_of(i * step, step)
        block = schur_ref[:owned, pl.ds(pl.multiple_of(owned + at, 128), step)]
        total_ref[:, pl.ds(at, step)] = jnp.dot(vector, block, preferred_element_type=F32)


def of_dim(dim, got):
    return jnp.concatenate(sides_of([ref[...] for ref in got], dim), axis=1)


def rows_of(dim, row, owned):
    start = owned + dim * row.shape[1]
    return slice(start, start + row.shape[1])


def some_rows_kernel(*refs):
    got, (sofar_ref, schur_ref, total_ref) = refs[:4], refs[4:]
    wide = total_ref.shape[1]
    owned = schur_ref.shape[1] - wide
    parts = [(dim, of_dim(dim, got[2 * i : 2 * i + 2])) for i, dim in enumerate(EARLY)]
    step = wide // 3

    @pl.loop(0, 3)
    def _(i):
        at = pl.multiple_of(i * step, step)
        columns = pl.ds(pl.multiple_of(owned + at, 128), step)
        here = pl.ds(at, step)
        total = sofar_ref[:, here]
        for dim, row in parts:
            block = schur_ref[rows_of(dim, row, owned), columns]
            total = total + jnp.dot(row, block, preferred_element_type=F32)
        total_ref[:, here] = total


def last_rows_kernel(*refs):
    got, (sofar_ref, schur_ref), slot_refs = refs[:2], refs[2:4], refs[4:]
    owned = schur_ref.shape[1] - sofar_ref.shape[1]
    row = of_dim(LATE, got[::-1])
    block = schur_ref[rows_of(LATE, row, owned), owned:]
    total = sofar_ref[...] + jnp.dot(row, block, preferred_element_type=F32)
    put_split(by_slot(joined(total)), slot_refs)


def own_columns_kernel(*refs):
    vector_ref, got, schur_ref, own_ref = refs[0], slot_order(refs[1:7]), refs[7], refs[8]
    owned = vector_ref.shape[1]
    row = jnp.concatenate(
        [split(vector_ref[...])] + [of_dim(dim, got[2 * dim : 2 * dim + 2]) for dim in range(3)],
        axis=1,
    )
    step = owned // 2

    @pl.loop(0, 2)
    def _(i):
        columns = pl.ds(pl.multiple_of(i * step, step), step)
        own_ref[:, columns] = joined(
            jnp.dot(row, schur_ref[:, columns], preferred_element_type=F32)
        )


def gram_entries(basis):
    rows = basis[0].shape[0]
    lane = lax.broadcasted_iota(jnp.int32, (rows, 128), 1)
    total = jnp.zeros((rows, 128), F32)
    newest = len(basis) - 1
    for i, vector in enumerate(basis):
        value = jnp.sum(vector * basis[newest], axis=1, keepdims=True)
        total = total + jnp.where(lane == i * 4 + newest, value, 0.0)
    return total


def next_kernel(*refs):
    sum_ref, got, places_ref, restricted_ref = refs[0], refs[1:3], refs[3], refs[4]
    vector_ref, next_ref, slot_refs = refs[5], refs[6], refs[7:]
    vector = (sum_ref[...] + added(ORDER[4:], got, places_ref)) * SCALE
    vector_ref[...] = vector
    products = joined(jnp.dot(split(vector), restricted_ref[...], preferred_element_type=F32))
    owned = vector.shape[1]
    next_ref[...] = products[:, :owned]
    put_split(by_slot(products[:, owned:]), slot_refs)


def gram_kernel(*refs):
    sum_ref, got, places_ref = refs[0], refs[1:3], refs[3]
    older, gram_ref = refs[4:-1], refs[-1]
    last = (sum_ref[...] + added(ORDER[4:], got, places_ref)) * SCALE
    basis = [ref[...] for ref in older] + [last]
    total = gram_entries(basis[:1])
    for newest in range(1, len(basis)):
        total = total + gram_entries(basis[: newest + 1])
    half = total.shape[0] // 2
    gram_ref[...] = total[:half] + pltpu.roll(total[half:], 64, 1)


def rotate_solve(columns, beta_norm):
    num_cols = len(columns)
    rhs_vec = [beta_norm] + [jnp.zeros_like(beta_norm) for unused in range(num_cols)]
    cosines = []
    sines = []
    triangle = []
    for section in range(num_cols):
        column = [columns[section][row_at] for row_at in range(section + 2)]
        for earlier in range(section):
            rotated_a = cosines[earlier] * column[earlier] + sines[earlier] * column[earlier + 1]
            rotated_b = -sines[earlier] * column[earlier] + cosines[earlier] * column[earlier + 1]
            column[earlier] = rotated_a
            column[earlier + 1] = rotated_b
        inverse = lax.rsqrt(
            column[section] * column[section] + column[section + 1] * column[section + 1]
        )
        cosine = column[section] * inverse
        sine_val = column[section + 1] * inverse
        column[section] = inverse
        cosines.append(cosine)
        sines.append(sine_val)
        rhs_vec[section + 1] = -sine_val * rhs_vec[section]
        rhs_vec[section] = cosine * rhs_vec[section]
        triangle.append(column[: section + 1])
    coeffs = [None] * num_cols
    for section in reversed(range(num_cols)):
        running = rhs_vec[section]
        for onward in range(section + 1, num_cols):
            running = running - triangle[onward][section] * coeffs[onward]
        coeffs[section] = running * triangle[section][section]
    return (coeffs, jnp.abs(rhs_vec[num_cols]))


def combine(gram):
    square = gram(0, 0) + EPSILON
    inverse_beta = lax.rsqrt(square)
    beta = square * inverse_beta
    made_of = [[inverse_beta]]
    columns = []
    for k in range(ITERS):
        applied = [None] + [c * (1.0 / SCALE) for c in made_of[k]]
        against = [
            functools.reduce(
                jnp.add, [gram(a, b) * applied[b] for b in range(1, k + 2)]
            )
            for a in range(k + 1)
        ]
        heights = [
            functools.reduce(jnp.add, [made_of[j][a] * against[a] for a in range(j + 1)])
            for j in range(k + 1)
        ]
        rest = [jnp.zeros_like(beta)] + applied[1:]
        for j in range(k + 1):
            for a in range(j + 1):
                rest[a] = rest[a] - heights[j] * made_of[j][a]
        square = jnp.zeros_like(beta)
        for a in range(k + 2):
            square = square + rest[a] * functools.reduce(
                jnp.add, [gram(a, b) * rest[b] for b in range(k + 2)]
            )
        square = jnp.maximum(square, 0.0) + EPSILON
        inverse = lax.rsqrt(square)
        columns.append(heights + [square * inverse])
        made_of.append([r * inverse for r in rest])
    weights, remainder = rotate_solve(columns, beta)
    shares = [
        functools.reduce(jnp.add, [weights[k] * made_of[k][i] for k in range(i, ITERS)])
        for i in range(ITERS)
    ]
    return shares, remainder * inverse_beta


def last_kernel(*refs):
    gram_ref, directions = refs[0], refs[1:-2]
    adjoint_ref, ratio_ref = refs[-2:]
    packed = gram_ref[...]
    sums = jnp.concatenate([packed, pltpu.roll(packed, 64, 1)], axis=0)

    def gram(a, b):
        at = min(a, b) * 4 + max(a, b)
        return sums[:, at : at + 1]

    shares, ratio = combine(gram)
    total = shares[0] * directions[0][...]
    for i in range(1, ITERS):
        total = total + shares[i] * directions[i][...]
    adjoint_ref[...] = total
    rows = ratio.shape[0]
    here = lax.broadcasted_iota(jnp.int32, (rows, rows), 0)
    there = lax.broadcasted_iota(jnp.int32, (rows, rows), 1)
    ratio_ref[...] = jnp.sum(jnp.where(here == there, ratio, 0.0), axis=0, keepdims=True)


def call(kernel, operands, outputs, name, keep=True, scratch=(), limit=8 << 20):
    space = pltpu.HBM if scratch else VMEM
    make = VMEM if keep else jax.ShapeDtypeStruct
    operands = [pltpu.with_memory_space_constraint(x, space) for x in operands]
    return pl.pallas_call(
        kernel,
        out_shape=tuple(make(shape, dtype) for shape, dtype in outputs),
        in_specs=[pl.BlockSpec(memory_space=space)] * len(operands),
        out_specs=tuple(pl.BlockSpec(memory_space=VMEM) for _ in outputs),
        scratch_shapes=scratch,
        compiler_params=pltpu.CompilerParams(vmem_limit_bytes=limit),
        cost_estimate=pl.CostEstimate(
            flops=0,
            bytes_accessed=sum(x.size * x.dtype.itemsize for x in operands),
            transcendentals=0,
        ),
        name=name,
    )(*operands)


def all_sum(array, stages):
    for axis in stages:
        n = lax.axis_size(axis)
        spread = jnp.broadcast_to(array[None], (n,) + array.shape)
        array = jnp.sum(lax.all_to_all(spread, axis, 0, 0), axis=0)
    return array


def local(gradient, local_schur, inverse_rows, face_maps):
    vector = gradient[0, 0, 0]
    schur = local_schur[0, 0, 0]
    restricted = inverse_rows[0, 0, 0]
    rows, owned = vector.shape
    width = face_maps.shape[-1]
    maps = face_maps.reshape(6, 1, width)

    block = ((rows, owned), F32)
    wide = ((2 * rows, 6 * width), F32)
    parcel = ((2 * rows, width), BF16)
    own, *slots = call(
        first_kernel,
        (maps, vector, restricted),
        (block,) + (((rows + 8, width), F32),) * 6,
        "first",
        scratch=[
            VMEM(maps.shape, maps.dtype),
            VMEM(vector.shape, vector.dtype),
            VMEM(restricted.shape, restricted.dtype),
            pltpu.SemaphoreType.DMA((3,)),
        ],
    )
    basis = [vector]
    directions = []
    for section in range(ITERS):
        if section == 0:
            (own,) = call(hold_kernel, (own, schur), (block,), "hold")
        got = trade(slots)
        if section == 0:
            parcels = got
            direction, picks, *slots = call(
                meet_kernel,
                (own, *ordered(got)),
                (block, ((owned, 6 * width), BF16)) + (parcel,) * 6,
                "meet",
            )
        else:
            got = ordered(got)
            (own,) = call(early_kernel, (own, *got[:4], places), (block,), "early")
            direction, *slots = call(
                direction_kernel, (own, *got[4:], places, picks), (block,) + (parcel,) * 6,
                "direction",
            )
        directions.append(direction)
        got = trade(slots)
        (total,) = call(own_rows_kernel, (direction, schur), (wide,), "own_rows")
        early = [got[2 * dim + side] for dim in EARLY for side in range(2)]
        late = [got[2 * LATE + 1], got[2 * LATE]]
        (total,) = call(some_rows_kernel, (*early, total, schur), (wide,), "some_rows")
        slots = call(last_rows_kernel, (*late, total, schur), (parcel,) * 6, "last_rows")
        (own,) = call(
            own_columns_kernel, (direction, *ordered(got), schur), (block,), "own_columns"
        )
        if section == 0:
            (places,) = call(
                turn_kernel, (*parcels, slots[0]), (((6 * width, owned), BF16),), "turn"
            )
        got = ordered(trade(slots))
        (own,) = call(early_kernel, (own, *got[:4], places), (block,), "early")
        if section + 1 < ITERS:
            vector, own, *slots = call(
                next_kernel,
                (own, *got[4:], places, restricted),
                (block,) * 2 + (parcel,) * 6,
                "next",
            )
            basis.append(vector)
    (gram,) = call(
        gram_kernel, (own, *got[4:], places, *basis), (((rows // 2, 128), F32),), "gram"
    )
    gram = all_sum(gram, (("gx", "gy"), "gz"))
    adjoint, ratio = call(
        last_kernel, (gram, *directions), (block, ((1, rows), F32)), "last", keep=False
    )
    return (adjoint[None, None, None], ratio.reshape(rows))


def solution(mesh):
    placed = P("gx", "gy", "gz", None, None)
    return jax.shard_map(
        local,
        mesh=mesh,
        in_specs=(placed,) * 4,
        out_specs=(placed, P()),
        check_vma=False,
    )
```

```python
import functools

import jax
import jax.numpy as jnp
import numpy as np
from jax import lax
from jax.experimental import pallas as pl
from jax.experimental.pallas import tpu as pltpu
from jax.sharding import PartitionSpec as P

ITERS = 3
EPSILON = 1e-06
SCALE = 2.0**-12
AXES = ("gx", "gy", "gz")
ASIDE = (1, 0, 1)
ORDER = (4, 5, 0, 1, 3, 2)
EARLY = (2, 0)
LATE = 1
BF16 = jnp.bfloat16
F32 = jnp.float32
VMEM = pltpu.VMEM


def partners(slot):
    dim = slot // 2
    sizes = [lax.axis_size(axis) for axis in AXES]
    pairs = []
    for place in np.ndindex(*sizes):
        at = list(place)
        step = 1 if (at[dim] - slot) % 2 == 0 else -1
        if 0 <= at[dim] + step < sizes[dim]:
            at[dim] += step
        else:
            beside = ASIDE[dim]
            at[beside] += 1 - 2 * (at[beside] % 2)
        pairs.append(
            tuple(int(np.ravel_multi_index(position, sizes)) for position in (place, at))
        )
    return pairs


def trade(slots):
    return [lax.ppermute(slots[slot], AXES, partners(slot)) for slot in range(6)]


def even_at(dim):
    return lax.rem(lax.axis_index(AXES[dim]), 2) == 0


def sides_of(pair, dim):
    even, odd = pair
    here = even_at(dim)
    return jnp.where(here, odd, even), jnp.where(here, even, odd)


def meets(slot):
    at = lax.axis_index(AXES[slot // 2])
    if slot % 2 == 0:
        return at >= 0
    return jnp.logical_and(at > 0, at < lax.axis_size(AXES[slot // 2]) - 1)


def split(x):
    high = x.astype(BF16)
    low = (x - high.astype(F32)).astype(BF16)
    return jnp.concatenate([high, low], axis=0)


def joined(x):
    rows = x.shape[0] // 2
    return x[:rows] + x[rows:]


def ordered(got):
    return [got[slot] for slot in ORDER]


def slot_order(got):
    return [got[ORDER.index(slot)] for slot in range(6)]


def by_slot(products):
    width = products.shape[1] // 6
    blocks = [products[:, face * width : (face + 1) * width] for face in range(6)]
    slots = []
    for dim in range(3):
        slots += sides_of((blocks[2 * dim], blocks[2 * dim + 1]), dim)
    return slots


def put_split(slots, refs):
    for block, ref in zip(slots, refs):
        ref[...] = split(block)


def first_kernel(*refs):
    sources, own_ref, slot_refs, scratch = refs[:3], refs[3], refs[4:10], refs[10:]
    maps_ref, vector_ref, restricted_ref, sems = scratch
    copies = [
        pltpu.make_async_copy(source, target, sems.at[i])
        for i, (source, target) in enumerate(zip(sources, scratch[:3]))
    ]
    for copy in copies:
        copy.start()
    for copy in copies:
        copy.wait()
    rows, owned = vector_ref.shape
    products = joined(
        jnp.dot(split(vector_ref[...]), restricted_ref[...], preferred_element_type=F32)
    )
    own_ref[...] = products[:, :owned]
    maps = jnp.concatenate([maps_ref[face].astype(F32) for face in range(6)], axis=1)
    maps = jnp.broadcast_to(maps, (8, maps.shape[1]))
    for block, row, ref in zip(by_slot(products[:, owned:]), by_slot(maps), slot_refs):
        ref[:rows] = block
        ref[rows:] = row


def added(slots, got, places_ref):
    width = got[0].shape[1]
    total = None
    for slot, part in zip(slots, got):
        place = places_ref[slot * width : (slot + 1) * width, :]
        product = jnp.dot(part[...], place, preferred_element_type=F32)
        total = product if total is None else total + product
    return joined(total)


def early_kernel(*refs):
    own_ref, got, places_ref, sum_ref = refs[0], refs[1:5], refs[5], refs[6]
    sum_ref[...] = own_ref[...] + added(ORDER[:4], got, places_ref)


def turn_kernel(*refs):
    got, places_ref = refs[:6], refs[7]
    width = got[0].shape[1]
    owned = places_ref.shape[1]
    place = lax.broadcasted_iota(jnp.int32, (width, owned), 1)
    for slot in range(6):
        column = jnp.transpose(got[slot][got[slot].shape[0] - 8 :, :])[:, :1].astype(jnp.int32)
        wanted = jnp.where(meets(slot), column, -1)
        places_ref[slot * width : (slot + 1) * width, :] = jnp.where(
            wanted == place, 1.0, 0.0
        ).astype(BF16)


def offer(vector, picks_ref, slot_refs):
    taken = jnp.dot(split(vector), picks_ref[...], preferred_element_type=F32).astype(BF16)
    width = taken.shape[1] // 6
    for slot in range(6):
        slot_refs[slot][...] = taken[:, slot * width : (slot + 1) * width]


def meet_kernel(*refs):
    own_ref, got, direction_ref, picks_ref = refs[0], slot_order(refs[1:7]), refs[7], refs[8]
    rows, owned = own_ref.shape
    width = got[0].shape[1]
    place = lax.broadcasted_iota(jnp.int32, (owned, width), 0)
    for slot in range(6):
        row = got[slot][rows : rows + 1, :].astype(jnp.int32)
        wanted = jnp.where(meets(slot), row, -1)
        picks_ref[:, slot * width : (slot + 1) * width] = jnp.where(
            wanted == place, 1.0, 0.0
        ).astype(BF16)
    parts = jnp.concatenate([split(ref[:rows]) for ref in got], axis=1)
    direction = own_ref[...] + joined(
        lax.dot_general(
            parts, picks_ref[...], (((1,), (1,)), ((), ())), preferred_element_type=F32
        )
    )
    direction_ref[...] = direction
    offer(direction, picks_ref, refs[9:])


def direction_kernel(*refs):
    sum_ref, got, places_ref, picks_ref, direction_ref = refs[0], refs[1:3], *refs[3:6]
    direction = sum_ref[...] + added(ORDER[4:], got, places_ref)
    direction_ref[...] = direction
    offer(direction, picks_ref, refs[6:])


def hold_kernel(own_ref, schur_ref, out_ref):
    out_ref[...] = own_ref[...]


def own_rows_kernel(vector_ref, schur_ref, total_ref):
    owned = vector_ref.shape[1]
    vector = split(vector_ref[...])
    step = total_ref.shape[1] // 2

    @pl.loop(0, 2)
    def _(i):
        at = pl.multiple_of(i * step, step)
        block = schur_ref[:owned, pl.ds(pl.multiple_of(owned + at, 128), step)]
        total_ref[:, pl.ds(at, step)] = jnp.dot(vector, block, preferred_element_type=F32)


def of_dim(dim, got):
    return jnp.concatenate(sides_of([ref[...] for ref in got], dim), axis=1)


def rows_of(dim, row, owned):
    start = owned + dim * row.shape[1]
    return slice(start, start + row.shape[1])


def some_rows_kernel(*refs):
    got, (sofar_ref, schur_ref, total_ref) = refs[:4], refs[4:]
    wide = total_ref.shape[1]
    owned = schur_ref.shape[1] - wide
    parts = [(dim, of_dim(dim, got[2 * i : 2 * i + 2])) for i, dim in enumerate(EARLY)]
    step = wide // 3

    @pl.loop(0, 3)
    def _(i):
        at = pl.multiple_of(i * step, step)
        columns = pl.ds(pl.multiple_of(owned + at, 128), step)
        here = pl.ds(at, step)
        total = sofar_ref[:, here]
        for dim, row in parts:
            block = schur_ref[rows_of(dim, row, owned), columns]
            total = total + jnp.dot(row, block, preferred_element_type=F32)
        total_ref[:, here] = total


def last_rows_kernel(*refs):
    got, (sofar_ref, schur_ref), slot_refs = refs[:2], refs[2:4], refs[4:]
    owned = schur_ref.shape[1] - sofar_ref.shape[1]
    row = of_dim(LATE, got[::-1])
    block = schur_ref[rows_of(LATE, row, owned), owned:]
    total = sofar_ref[...] + jnp.dot(row, block, preferred_element_type=F32)
    put_split(by_slot(joined(total)), slot_refs)


def own_columns_kernel(*refs):
    vector_ref, got, schur_ref, own_ref = refs[0], slot_order(refs[1:7]), refs[7], refs[8]
    owned = vector_ref.shape[1]
    row = jnp.concatenate(
        [split(vector_ref[...])] + [of_dim(dim, got[2 * dim : 2 * dim + 2]) for dim in range(3)],
        axis=1,
    )
    step = owned // 2

    @pl.loop(0, 2)
    def _(i):
        columns = pl.ds(pl.multiple_of(i * step, step), step)
        own_ref[:, columns] = joined(
            jnp.dot(row, schur_ref[:, columns], preferred_element_type=F32)
        )


def gram_entries(basis):
    rows = basis[0].shape[0]
    lane = lax.broadcasted_iota(jnp.int32, (rows, 128), 1)
    total = jnp.zeros((rows, 128), F32)
    newest = len(basis) - 1
    for i, vector in enumerate(basis):
        value = jnp.sum(vector * basis[newest], axis=1, keepdims=True)
        total = total + jnp.where(lane == i * 4 + newest, value, 0.0)
    return total


def next_kernel(*refs):
    sum_ref, got, places_ref, restricted_ref = refs[0], refs[1:3], refs[3], refs[4]
    vector_ref, slot_refs = refs[5], refs[6:]
    vector = (sum_ref[...] + added(ORDER[4:], got, places_ref)) * SCALE
    vector_ref[...] = vector
    faces = restricted_ref[:, vector.shape[1] :]
    put_split(by_slot(joined(jnp.dot(split(vector), faces, preferred_element_type=F32))), slot_refs)


def own_part_kernel(vector_ref, restricted_ref, own_ref):
    owned = vector_ref.shape[1]
    own_ref[...] = joined(
        jnp.dot(split(vector_ref[...]), restricted_ref[:, :owned], preferred_element_type=F32)
    )


def gram_kernel(*refs):
    sum_ref, got, places_ref = refs[0], refs[1:3], refs[3]
    older, gram_ref = refs[4:-1], refs[-1]
    last = (sum_ref[...] + added(ORDER[4:], got, places_ref)) * SCALE
    basis = [ref[...] for ref in older] + [last]
    total = gram_entries(basis[:1])
    for newest in range(1, len(basis)):
        total = total + gram_entries(basis[: newest + 1])
    half = total.shape[0] // 2
    gram_ref[...] = total[:half] + pltpu.roll(total[half:], 64, 1)


def rotate_solve(columns, beta_norm):
    num_cols = len(columns)
    rhs_vec = [beta_norm] + [jnp.zeros_like(beta_norm) for unused in range(num_cols)]
    cosines = []
    sines = []
    triangle = []
    for section in range(num_cols):
        column = [columns[section][row_at] for row_at in range(section + 2)]
        for earlier in range(section):
            rotated_a = cosines[earlier] * column[earlier] + sines[earlier] * column[earlier + 1]
            rotated_b = -sines[earlier] * column[earlier] + cosines[earlier] * column[earlier + 1]
            column[earlier] = rotated_a
            column[earlier + 1] = rotated_b
        inverse = lax.rsqrt(
            column[section] * column[section] + column[section + 1] * column[section + 1]
        )
        cosine = column[section] * inverse
        sine_val = column[section + 1] * inverse
        column[section] = inverse
        cosines.append(cosine)
        sines.append(sine_val)
        rhs_vec[section + 1] = -sine_val * rhs_vec[section]
        rhs_vec[section] = cosine * rhs_vec[section]
        triangle.append(column[: section + 1])
    coeffs = [None] * num_cols
    for section in reversed(range(num_cols)):
        running = rhs_vec[section]
        for onward in range(section + 1, num_cols):
            running = running - triangle[onward][section] * coeffs[onward]
        coeffs[section] = running * triangle[section][section]
    return (coeffs, jnp.abs(rhs_vec[num_cols]))


def combine(gram):
    square = gram(0, 0) + EPSILON
    inverse_beta = lax.rsqrt(square)
    beta = square * inverse_beta
    made_of = [[inverse_beta]]
    columns = []
    for k in range(ITERS):
        applied = [None] + [c * (1.0 / SCALE) for c in made_of[k]]
        against = [
            functools.reduce(
                jnp.add, [gram(a, b) * applied[b] for b in range(1, k + 2)]
            )
            for a in range(k + 1)
        ]
        heights = [
            functools.reduce(jnp.add, [made_of[j][a] * against[a] for a in range(j + 1)])
            for j in range(k + 1)
        ]
        rest = [jnp.zeros_like(beta)] + applied[1:]
        for j in range(k + 1):
            for a in range(j + 1):
                rest[a] = rest[a] - heights[j] * made_of[j][a]
        square = jnp.zeros_like(beta)
        for a in range(k + 2):
            square = square + rest[a] * functools.reduce(
                jnp.add, [gram(a, b) * rest[b] for b in range(k + 2)]
            )
        square = jnp.maximum(square, 0.0) + EPSILON
        inverse = lax.rsqrt(square)
        columns.append(heights + [square * inverse])
        made_of.append([r * inverse for r in rest])
    weights, remainder = rotate_solve(columns, beta)
    shares = [
        functools.reduce(jnp.add, [weights[k] * made_of[k][i] for k in range(i, ITERS)])
        for i in range(ITERS)
    ]
    return shares, remainder * inverse_beta


def last_kernel(*refs):
    gram_ref, directions = refs[0], refs[1:-2]
    adjoint_ref, ratio_ref = refs[-2:]
    packed = gram_ref[...]
    sums = jnp.concatenate([packed, pltpu.roll(packed, 64, 1)], axis=0)

    def gram(a, b):
        at = min(a, b) * 4 + max(a, b)
        return sums[:, at : at + 1]

    shares, ratio = combine(gram)
    total = shares[0] * directions[0][...]
    for i in range(1, ITERS):
        total = total + shares[i] * directions[i][...]
    adjoint_ref[...] = total
    rows = ratio.shape[0]
    here = lax.broadcasted_iota(jnp.int32, (rows, rows), 0)
    there = lax.broadcasted_iota(jnp.int32, (rows, rows), 1)
    ratio_ref[...] = jnp.sum(jnp.where(here == there, ratio, 0.0), axis=0, keepdims=True)


def call(kernel, operands, outputs, name, keep=True, scratch=(), limit=8 << 20):
    space = pltpu.HBM if scratch else VMEM
    make = VMEM if keep else jax.ShapeDtypeStruct
    operands = [pltpu.with_memory_space_constraint(x, space) for x in operands]
    return pl.pallas_call(
        kernel,
        out_shape=tuple(make(shape, dtype) for shape, dtype in outputs),
        in_specs=[pl.BlockSpec(memory_space=space)] * len(operands),
        out_specs=tuple(pl.BlockSpec(memory_space=VMEM) for _ in outputs),
        scratch_shapes=scratch,
        compiler_params=pltpu.CompilerParams(vmem_limit_bytes=limit),
        cost_estimate=pl.CostEstimate(
            flops=0,
            bytes_accessed=sum(x.size * x.dtype.itemsize for x in operands),
            transcendentals=0,
        ),
        name=name,
    )(*operands)


def all_sum(array, stages):
    for axis in stages:
        n = lax.axis_size(axis)
        spread = jnp.broadcast_to(array[None], (n,) + array.shape)
        array = jnp.sum(lax.all_to_all(spread, axis, 0, 0), axis=0)
    return array


def local(gradient, local_schur, inverse_rows, face_maps):
    vector = gradient[0, 0, 0]
    schur = local_schur[0, 0, 0]
    restricted = inverse_rows[0, 0, 0]
    rows, owned = vector.shape
    width = face_maps.shape[-1]
    maps = face_maps.reshape(6, 1, width)

    block = ((rows, owned), F32)
    wide = ((2 * rows, 6 * width), F32)
    parcel = ((2 * rows, width), BF16)
    own, *slots = call(
        first_kernel,
        (maps, vector, restricted),
        (block,) + (((rows + 8, width), F32),) * 6,
        "first",
        scratch=[
            VMEM(maps.shape, maps.dtype),
            VMEM(vector.shape, vector.dtype),
            VMEM(restricted.shape, restricted.dtype),
            pltpu.SemaphoreType.DMA((3,)),
        ],
    )
    basis = [vector]
    directions = []
    for section in range(ITERS):
        if section == 0:
            (own,) = call(hold_kernel, (own, schur), (block,), "hold")
        got = trade(slots)
        if section == 0:
            parcels = got
            direction, picks, *slots = call(
                meet_kernel,
                (own, *ordered(got)),
                (block, ((owned, 6 * width), BF16)) + (parcel,) * 6,
                "meet",
            )
        else:
            got = ordered(got)
            (own,) = call(early_kernel, (own, *got[:4], places), (block,), "early")
            direction, *slots = call(
                direction_kernel, (own, *got[4:], places, picks), (block,) + (parcel,) * 6,
                "direction",
            )
        directions.append(direction)
        got = trade(slots)
        (total,) = call(own_rows_kernel, (direction, schur), (wide,), "own_rows")
        early = [got[2 * dim + side] for dim in EARLY for side in range(2)]
        late = [got[2 * LATE + 1], got[2 * LATE]]
        (total,) = call(some_rows_kernel, (*early, total, schur), (wide,), "some_rows")
        slots = call(last_rows_kernel, (*late, total, schur), (parcel,) * 6, "last_rows")
        (own,) = call(
            own_columns_kernel, (direction, *ordered(got), schur), (block,), "own_columns"
        )
        if section == 0:
            (places,) = call(
                turn_kernel, (*parcels, slots[0]), (((6 * width, owned), BF16),), "turn"
            )
        got = ordered(trade(slots))
        (own,) = call(early_kernel, (own, *got[:4], places), (block,), "early")
        if section + 1 < ITERS:
            vector, *slots = call(
                next_kernel,
                (own, *got[4:], places, restricted),
                (block,) + (parcel,) * 6,
                "next",
            )
            (own,) = call(own_part_kernel, (vector, restricted), (block,), "own_part")
            basis.append(vector)
    (gram,) = call(
        gram_kernel, (own, *got[4:], places, *basis), (((rows // 2, 128), F32),), "gram"
    )
    gram = all_sum(gram, (("gx", "gy"), "gz"))
    adjoint, ratio = call(
        last_kernel, (gram, *directions), (block, ((1, rows), F32)), "last", keep=False
    )
    return (adjoint[None, None, None], ratio.reshape(rows))


def solution(mesh):
    placed = P("gx", "gy", "gz", None, None)
    return jax.shard_map(
        local,
        mesh=mesh,
        in_specs=(placed,) * 4,
        out_specs=(placed, P()),
        check_vma=False,
    )
```
